32 devices in a mesh: groups: 2 (over y), dp: 4 (over z), tm: 2 (over core), rows: 2 (over x).
Axes of the slice: x: 2, y: 2, z: 4, core: 2. Of those that a mesh axis runs over, the one named last changes fastest.
Arguments:
- spikes: bfloat16 [8, 6, 16, 64, 320], P(('groups', 'dp'), 'tm', 'rows'), parts along dimension 0, may hold values from 0 to 1, as said below
- cotangent: bfloat16 [8, 6, 16, 64, 320], P(('groups', 'dp'), 'tm', 'rows'), parts along dimension 0, may hold values from -6 to 6
- weight_codes: int32 [3, 3, 320, 320], P(None, None, None, 'dp'), may hold values from -127 to 127
- block_exponents: int32 [3, 3, 10, 320], P(None, None, None, 'dp'), may hold values from -13 to -11
- current_bias: float32 [320], replicated, may hold values from -3 to 3
- threshold: float32 [320], replicated, may hold values from 0.5 to 1.5
Outputs:
- residual_output: bfloat16 [8, 6, 16, 64, 320], P(('groups', 'dp'), 'tm', 'rows'), parts along dimension 0
- input_grad: float32 [8, 6, 16, 64, 320], P(('groups', 'dp'), 'tm', 'rows'), parts along dimension 0
The draws below stay inside these ranges and needn't reach their ends.
There are 2 independent parts, one for each index of `groups`. The reference program is written for one: setup_inputs(seed, part) draws one part's arguments, and reference() takes and returns one part's arrays. A program takes and returns all parts, laid end to end along the dimension named above; an argument that names none is the same for every part. Nothing has to cross between parts.
Inputs may be any that keep to these rules, and one draw needn't show every extreme that they name: `spikes`: every entry is 0 or 1.
All inputs are finite; a program needn't handle non-finite values.
Results may differ from the reference program's by a relative error of at most 0.002.
Values may be sent and summed in bfloat16 or wider, within the bound.
No kernel may reach another device: no remote copies, remote signals or barrier semaphores. Data moves between devices by JAX's collectives and lax.ppermute only.
A program may use at most 64 MiB of HBM per device.

```python
import math
import jax
import jax.numpy as jnp
from jax import lax

CH = 320
MX_BLOCK = 32
W = 64
B = 4
T_SIZE = 6
H = 16


def draw_spikes(key, part):
    chance = 0.3
    values = jax.random.bernoulli(key, chance, (B, T_SIZE, H, W, CH)).astype(jnp.float32)
    return values.astype(jnp.bfloat16)


def set_ends(result, own_key, low, top_value):
    place = [jax.random.randint(jax.random.fold_in(own_key, axis), (), 0, length) for axis, length in enumerate(result.shape)]
    main_axis = result.shape.index(max(result.shape))
    next_to = place[:main_axis] + [(place[main_axis] + 1) % result.shape[main_axis]] + place[main_axis + 1:]
    return result.at[tuple(place)].set(low).at[tuple(next_to)].set(top_value)


def steps_of(own_key, dims, shards, least, top_value):
    gain = 1.0
    for dim, blocks in shards:
        draws = jax.random.uniform(jax.random.fold_in(jax.random.fold_in(own_key, 6), dim), (blocks,), jnp.float32, least / len(shards), top_value / len(shards))
        gain = gain * jnp.repeat(jnp.exp(draws), dims[dim] // blocks).reshape((-1,) + (1,) * (len(dims) - 1 - dim))
    return gain


def noise(stream_key, shape, width, most, pieces=(), kind=jnp.bfloat16):
    loudness = steps_of(stream_key, shape, pieces, -0.22, 0.18) if pieces else 1.0
    values = jax.random.normal(stream_key, shape, jnp.float32) * width * loudness
    return jnp.minimum(jnp.maximum(values, -most), most).astype(kind)


def setup_inputs(seed: int = 0, part: int = 0) -> dict:
    key_of = jax.random.split(jax.random.key(seed), 7)
    part_keys = jax.random.split(jax.random.fold_in(key_of[6], part), 7)
    spikes = draw_spikes(jax.random.fold_in(jax.random.fold_in(key_of[6], part), 71), part)
    cotangent = noise(part_keys[1], (B, T_SIZE, H, W, CH), 1.0, 6.0, ((0, 4), (1, 2), (2, 2)))
    weight_codes = set_ends(jax.random.randint(key_of[2], (3, 3, CH, CH), -127, 128), jax.random.fold_in(key_of[2], 1), -127, 127).astype(jnp.int32)
    block_exponents = set_ends(jax.random.randint(key_of[3], (3, 3, CH // MX_BLOCK, CH), -13, -10), jax.random.fold_in(key_of[3], 1), -13, (-10) - 1).astype(jnp.int32)
    current_bias = noise(key_of[4], (CH,), 0.5, 3.0, (), jnp.float32)
    threshold = jnp.clip(jnp.exp(jax.random.uniform(key_of[5], (CH,), jnp.float32, math.log(0.5), math.log(1.5))), 0.5, 1.5)
    return dict(spikes=spikes, cotangent=cotangent, weight_codes=weight_codes, block_exponents=block_exponents, current_bias=current_bias, threshold=threshold)


surrogate_steepness = 2.0


def dequantize(weight_codes, block_exponents):
    scales = 1.0 / (2 ** (-block_exponents)).astype(jnp.float32)
    scales = jnp.repeat(scales, MX_BLOCK, axis=2)
    return (weight_codes.astype(jnp.float32) * scales).astype(jnp.bfloat16)


def reference(spikes, cotangent, weight_codes, block_exponents, current_bias, threshold):
    weight = dequantize(weight_codes, block_exponents).astype(jnp.float32)

    def one_sample(sample_pair):
        spike_raw, upstream_raw = sample_pair
        input_spikes = spike_raw.astype(jnp.float32)
        height = input_spikes.shape[1]
        columns = input_spikes.shape[2]
        padded = jnp.pad(input_spikes, ((0, 0), (1, 1), (1, 1), (0, 0)))
        input_current = jnp.zeros(input_spikes.shape, jnp.float32)
        for row_tap in range(3):
            for col_tap in range(3):
                input_current = input_current + jnp.einsum("thwi,io->thwo", padded[:, row_tap:row_tap + height, col_tap:col_tap + columns], weight[row_tap, col_tap])
        input_current = input_current + current_bias

        def step_forward(membrane_voltage, current_now):
            potential = membrane_voltage + current_now
            spiking = jax.nn.sigmoid(surrogate_steepness * (potential - threshold))
            return potential - threshold * spiking, spiking

        unused_value, fired_spikes = lax.scan(step_forward, jnp.zeros(input_spikes.shape[1:], jnp.float32), input_current)
        residual_output = (fired_spikes + input_spikes).astype(jnp.bfloat16)
        upstream = upstream_raw.astype(jnp.float32)
        surrogate_slopes = surrogate_steepness * fired_spikes * (1.0 - fired_spikes)
        drive_term = upstream * surrogate_slopes
        carry_gain = 1.0 - threshold * surrogate_slopes

        def retreat(adjoint_now, terms):
            updated = terms[0] + terms[1] * adjoint_now
            return updated, updated

        unused_value, current_grad = lax.scan(retreat, jnp.zeros(input_spikes.shape[1:], jnp.float32), (drive_term, carry_gain), reverse=True)
        grad_rounded = lax.optimization_barrier(current_grad.astype(jnp.bfloat16)).astype(jnp.float32)
        grad_padded = jnp.pad(grad_rounded, ((0, 0), (1, 1), (1, 1), (0, 0)))
        input_grad = upstream
        for row_tap in range(3):
            for col_tap in range(3):
                input_grad = input_grad + jnp.einsum("thwo,io->thwi", grad_padded[:, 2 - row_tap:2 - row_tap + height, 2 - col_tap:2 - col_tap + columns], weight[row_tap, col_tap])
        return residual_output, input_grad

    residual_output, input_grad = lax.map(one_sample, (spikes, cotangent))
    return (residual_output, input_grad)
```

```python
import functools

import jax
import jax.numpy as jnp
from jax import lax
from jax.experimental import pallas as pl
from jax.experimental.pallas import tpu as pltpu
from jax.sharding import PartitionSpec as P

MX_BLOCK = 32
TAPS = 3
F32 = jnp.float32
BF16 = jnp.bfloat16
VMEM_SPEC = pl.BlockSpec(memory_space=pltpu.VMEM)
ANY_SPEC = pl.BlockSpec(memory_space=pl.ANY)


def params(mib):
    return pltpu.CompilerParams(vmem_limit_bytes=mib << 20)


def dot(a, b, dims):
    return lax.dot_general(a, b, (dims, ((), ())), preferred_element_type=F32)


def dequant_kernel(codes_ref, exps_ref, out_ref):
    outs, ins = codes_ref.shape[2:]
    blocks = exps_ref.shape[1]
    spread = lax.broadcasted_iota(jnp.int32, (blocks, ins), 1) // MX_BLOCK
    spread = (spread == lax.broadcasted_iota(jnp.int32, (blocks, ins), 0)).astype(F32).astype(BF16)
    for dy in range(TAPS):
        parts = []
        for dx in range(TAPS):
            scale = 1.0 / lax.shift_left(jnp.int32(1), -exps_ref[dy, :, dx, :]).astype(F32)
            scale = dot(scale.astype(BF16), spread, ((0,), (0,)))
            parts.append(codes_ref[dy, dx].astype(F32) * scale)
        parts.append(jnp.zeros((outs, out_ref.shape[1] - TAPS * ins), F32))
        out_ref[dy * outs : (dy + 1) * outs, :] = jnp.concatenate(parts, axis=1).astype(BF16)


def dequantize(weight_codes, block_exponents, lanes):
    outs = weight_codes.shape[3]
    return pl.pallas_call(
        dequant_kernel,
        out_shape=jax.ShapeDtypeStruct((TAPS * outs, lanes), BF16),
        in_specs=[VMEM_SPEC] * 2,
        out_specs=VMEM_SPEC,
        compiler_params=params(16),
        name="dequant",
    )(weight_codes.transpose(0, 1, 3, 2), block_exponents.transpose(0, 2, 1, 3))


def strip_offsets(two, row):
    if two:
        return 1 + row, ((1 - row) * 0, row)
    return 2, None


def taps_kernel(two, spikes_ref, spikes2_ref, cot_ref, cot2_ref, *refs):
    n_halo = 1 if two else 2
    halos, halos2 = refs[:n_halo], refs[n_halo : 2 * n_halo]
    x_ref, s_ref, c_ref = refs[2 * n_halo :]
    core, row = lax.axis_index("tm"), lax.axis_index("rows")
    steps, rows, cols, ch = spikes_ref.shape
    half = ch // 2
    lanes = x_ref.shape[2]
    strip = x_ref.shape[0]
    edge = lax.broadcasted_iota(jnp.int32, (cols, 1), 0)

    def half_of(x):
        return jnp.where(core == 0, x[:, :half], x[:, half:])

    def put_taps(x, s, t):
        before = jnp.where(edge == 0, 0.0, pltpu.roll(x, 1, 0))
        after = jnp.where(edge == cols - 1, 0.0, pltpu.roll(x, cols - 1, 0))
        pad = jnp.zeros((cols, lanes - TAPS * ch), F32)
        x_ref[s, pl.ds(pl.multiple_of(t * cols, cols), cols), :] = jnp.concatenate([before, x, after, pad], axis=1).astype(BF16)

    own = 1 + row if two else 2
    first = own - 1
    for which, (s_in, c_in, h_in) in enumerate(((spikes_ref, cot_ref, halos), (spikes2_ref, cot2_ref, halos2))):

        def body(n, carry, s_in=s_in, c_in=c_in, which=which):
            t, h = n // rows, n % rows
            x = s_in[t, h].astype(F32)
            put_taps(x, own + h, which * steps + t)
            s_ref[first + h, which * steps + t] = half_of(x).astype(BF16)
            c_ref[first + h, which * steps + t] = half_of(c_in[t, h].astype(F32)).astype(BF16)
            return carry

        lax.fori_loop(0, steps * rows, body, 0)
        for side, halo in enumerate(h_in):
            if two:
                s0 = jnp.where(row == 0, rows + 1, 0)
                u0 = jnp.where(row == 0, rows, 0)
            else:
                s0, u0 = (0, 0) if side == 0 else (rows + 2, rows + 1)

            def halo_body(t, carry, halo=halo, s0=s0, u0=u0, which=which):
                for k in range(2):
                    put_taps(halo[t, k].astype(F32), s0 + k, which * steps + t)
                c_ref[u0, which * steps + t] = half_of(halo[t, 2].astype(F32)).astype(BF16)
                s_ref[u0, which * steps + t] = jnp.zeros((cols, half), BF16)
                return carry

            lax.fori_loop(0, steps, halo_body, 0)
    if two:
        x_ref[jnp.where(row == 0, 0, strip - 1)] = jnp.zeros(x_ref.shape[1:], BF16)


def build_taps(two, own, other, lanes):
    spikes, cot, halos = own
    steps, rows, cols, ch = spikes.shape
    n_cur = rows + 1 if two else rows + 2
    outs = (
        jax.ShapeDtypeStruct((n_cur + 2, 2 * steps * cols, lanes), BF16),
        jax.ShapeDtypeStruct((n_cur, 2 * steps, cols, ch // 2), BF16),
        jax.ShapeDtypeStruct((n_cur, 2 * steps, cols, ch // 2), BF16),
    )
    args = (spikes, other[0], cot, other[1], *halos, *other[2])
    return pl.pallas_call(
        functools.partial(taps_kernel, two),
        out_shape=outs,
        in_specs=[VMEM_SPEC] * len(args),
        out_specs=(VMEM_SPEC,) * 3,
        compiler_params=params(40),
        name="taps",
    )(*args)


def assemble(wh_ref, parts, place):
    outs = parts[0].shape[0] // TAPS
    half = wh_ref.shape[0] // TAPS
    for k, part in enumerate(parts):
        at = lax.rem(place + k, len(parts)) * outs if len(parts) > 1 else 0
        for dy in range(TAPS):
            start = dy * half + at
            if len(parts) > 1:
                start = pl.multiple_of(start, 16)
            wh_ref[pl.ds(start, outs), :] = part[dy * outs : (dy + 1) * outs, :]


def forward_kernel(two, n_parts, *refs):
    parts = refs[:n_parts]
    x_hbm, s_ref, c_ref, bias_ref, thr_ref, gk_ref, gs_ref, rk_ref, rs_ref, wh_ref, xs, cur_ref, sems = refs[n_parts:]
    core, row = lax.axis_index("tm"), lax.axis_index("rows")
    place = lax.rem(lax.axis_index("dp"), n_parts)
    strip = xs.shape[0]
    n_cur, times, cols, half = s_ref.shape
    steps = times // 2

    def copy(s):
        return pltpu.make_async_copy(x_hbm.at[s], xs.at[s], sems.at[s])

    for s in range(strip):
        copy(s).start()
    assemble(wh_ref, parts, place)
    bias = jnp.where(core == 0, bias_ref[:, :half], bias_ref[:, half:])
    thr = jnp.where(core == 0, thr_ref[:, :half], thr_ref[:, half:])

    def currents(u):
        total = None
        for dy in range(TAPS):
            term = dot(xs[u + dy], wh_ref[dy * half : (dy + 1) * half, :], ((1,), (1,)))
            total = term if total is None else total + term
        cur_ref[lax.rem(u, 2)] = total + bias

    chunk = 16

    def scan(u):
        slot = lax.rem(u, 2)
        g = u + 1 - row if two else u
        inside = None
        if not two:
            last = lax.axis_size("rows") - 1
            inside = jnp.where(((u == 0) & (row == 0)) | ((u == n_cur - 1) & (row == last)), 0.0, 1.0)
        for w0 in range(0, cols, chunk):
            state = jnp.zeros((chunk, half), F32)
            fired, where_t = [], []
            for t in range(times):
                part, tl = divmod(t, steps)
                at = lax.rem(core + part, 2) * steps + tl
                where_t.append(at)
                now = cur_ref[slot, pl.ds(pl.multiple_of(at * cols + w0, chunk), chunk), :]
                potential = state + now
                spiking = 0.5 + 0.5 * jnp.tanh(potential - thr)
                state = potential - thr * spiking
                fired.append(spiking)
            res = [(f + s_ref[u, at, w0 : w0 + chunk, :].astype(F32)).astype(BF16) for f, at in zip(fired, where_t)]
            adjoint = jnp.zeros((chunk, half), F32)
            grads = [None] * times
            for t in reversed(range(times)):
                slope = 2.0 * fired[t] * (1.0 - fired[t])
                drive = c_ref[u, where_t[t], w0 : w0 + chunk, :].astype(F32) * slope
                adjoint = drive + (1.0 - thr * slope) * adjoint
                out = adjoint if inside is None else adjoint * inside
                grads[t] = out.astype(BF16)
            mine = core == 0
            for tl in range(steps):
                a, b = grads[tl], grads[steps + tl]
                gk_ref[tl, g, w0 : w0 + chunk, :] = jnp.where(mine, a, b)
                gs_ref[tl, g, w0 : w0 + chunk, :] = jnp.where(mine, b, a)
                a, b = res[tl], res[steps + tl]
                rk_ref[tl, u, w0 : w0 + chunk, :] = jnp.where(mine, a, b)
                rs_ref[tl, u, w0 : w0 + chunk, :] = jnp.where(mine, b, a)

    if two:
        edge = jnp.where(row == 0, 0, gk_ref.shape[1] - 1)
        for ref in (gk_ref, gs_ref):
            for tl in range(steps):
                ref[tl, edge] = jnp.zeros((cols, half), BF16)
    for s in range(TAPS):
        copy(s).wait()
    currents(jnp.int32(0))

    def body(u, carry):
        copy(u + TAPS).wait()
        currents(u + 1)
        scan(u)
        return carry

    lax.fori_loop(0, n_cur - 1, body, 0)
    scan(jnp.int32(n_cur - 1))


def forward(two, parts, taps, bias, thr):
    x, s, c = taps
    strip, positions, lanes = x.shape
    n_cur, times, cols, half = s.shape
    steps = times // 2
    rows = n_cur - 1 if two else n_cur - 2
    grad = jax.ShapeDtypeStruct((steps, rows + 2, cols, half), BF16)
    res = jax.ShapeDtypeStruct((steps, n_cur, cols, half), BF16)
    return pl.pallas_call(
        functools.partial(forward_kernel, two, len(parts)),
        out_shape=(grad, grad, res, res),
        in_specs=[VMEM_SPEC] * len(parts) + [ANY_SPEC] + [VMEM_SPEC] * 4,
        out_specs=(VMEM_SPEC,) * 4,
        scratch_shapes=[
            pltpu.VMEM((TAPS * half, lanes), BF16),
            pltpu.VMEM((strip, positions, lanes), BF16),
            pltpu.VMEM((2, positions, half), F32),
            pltpu.SemaphoreType.DMA((strip,)),
        ],
        compiler_params=params(40),
        name="forward",
    )(*parts, x, s, c, bias, thr)


def backward_kernel(n_parts, with_res, two, *refs):
    parts = refs[:n_parts]
    if with_res:
        g_ref, base_ref, rk_ref, rs_ref, out_ref, res_ref, wh_ref = refs[n_parts:]
    else:
        g_ref, base_ref, out_ref, wh_ref = refs[n_parts:]
    steps, rows2, cols, half = g_ref.shape
    rows, ch = rows2 - 2, base_ref.shape[3]
    core, row = lax.axis_index("tm"), lax.axis_index("rows")
    assemble(wh_ref, parts, lax.rem(lax.axis_index("dp"), n_parts))
    edge = lax.broadcasted_iota(jnp.int32, (1, cols, 1), 1)
    block = 4

    def body(n, carry):
        t, h0 = n // (rows // block), n % (rows // block) * block
        total = None
        for dy in range(TAPS):
            grads = g_ref[t, pl.ds(h0 + 2 - dy, block)].reshape(block * cols, half)
            term = dot(grads, wh_ref[dy * half : (dy + 1) * half, :], ((1,), (0,)))
            total = term if total is None else total + term
        total = total.reshape(block, cols, -1)
        left, mid, right = (total[:, :, k * ch : (k + 1) * ch] for k in range(TAPS))
        left = jnp.where(edge == cols - 1, 0.0, pltpu.roll(left, cols - 1, 1))
        right = jnp.where(edge == 0, 0.0, pltpu.roll(right, 1, 1))
        out_ref[t, pl.ds(h0, block)] = base_ref[t, pl.ds(h0, block)].astype(F32) + (left + mid + right)
        if with_res:
            first = row if two else 1
            a = rk_ref[t, pl.ds(h0 + first, block)].astype(F32)
            b = rs_ref[t, pl.ds(h0 + first, block)].astype(F32)
            both = jnp.concatenate([jnp.where(core == 0, a, b), jnp.where(core == 0, b, a)], axis=2)
            res_ref[t, pl.ds(h0, block)] = both.astype(BF16)
        return carry

    lax.fori_loop(0, steps * (rows // block), body, 0)


def backward(two, parts, grads, base, res=()):
    steps, rows, cols, ch = base.shape
    half = grads.shape[3]
    out = [jax.ShapeDtypeStruct(base.shape, F32)]
    if res:
        out.append(jax.ShapeDtypeStruct(base.shape, BF16))
    return pl.pallas_call(
        functools.partial(backward_kernel, len(parts), bool(res), two),
        out_shape=tuple(out),
        in_specs=[VMEM_SPEC] * (len(parts) + 2 + len(res)),
        out_specs=(VMEM_SPEC,) * len(out),
        scratch_shapes=[pltpu.VMEM((TAPS * half, parts[0].shape[1]), BF16)],
        compiler_params=params(40),
        name="backward_own" if not res else "backward_other",
    )(*parts, grads, base, *res)


def swap_cores(x):
    return lax.ppermute(x, "tm", [(0, 1), (1, 0)])


def fetch_halos(spikes, cot):
    count = lax.axis_size("rows")
    rows = spikes.shape[1]
    row = lax.axis_index("rows")
    if count == 2:
        s = lax.dynamic_slice_in_dim(spikes, (1 - row) * (rows - 2), 2, axis=1)
        c = lax.dynamic_slice_in_dim(cot, (1 - row) * (rows - 1), 1, axis=1)
        return [lax.ppermute(jnp.concatenate([s, c], axis=1), "rows", [(0, 1), (1, 0)])]
    tail = jnp.concatenate([spikes[:, rows - 2 :], cot[:, rows - 1 :]], axis=1)
    head = jnp.concatenate([spikes[:, :2], cot[:, :1]], axis=1)
    return [
        lax.ppermute(tail, "rows", [(i, i + 1) for i in range(count - 1)]),
        lax.ppermute(head, "rows", [(i + 1, i) for i in range(count - 1)]),
    ]


def fetch_weights(shard):
    count = lax.axis_size("dp")
    h = count // 2
    rounds = []
    for k in range(h):
        pairs = []
        for z in range(count):
            for c in range(2):
                s = c * h + (z + k) % h
                pairs.append((s * 2 + z // h, z * 2 + c))
        rounds.append(lax.ppermute(shard, ("dp", "tm"), pairs))
    return rounds


def in_order(rounds):
    h = len(rounds)
    outs = rounds[0].shape[0] // TAPS
    lanes = rounds[0].shape[1]
    if outs % 16 == 0:
        return rounds
    stack = jnp.stack([r.reshape(TAPS, outs, lanes) for r in rounds], axis=1)
    stack = jnp.roll(stack, lax.axis_index("dp") % h, axis=1)
    return [stack.reshape(TAPS * h * outs, lanes)]


def on_device(spikes, cotangent, weight_codes, block_exponents, current_bias, threshold):
    ch = spikes.shape[-1]
    lanes = -(-TAPS * ch // 256) * 256
    two = lax.axis_size("rows") == 2
    spikes, cot = spikes[0], cotangent[0]
    halos = fetch_halos(spikes, cot)
    shard = dequantize(weight_codes, block_exponents, lanes)
    own = (spikes, cot, halos)
    other = (swap_cores(spikes), swap_cores(cot), [swap_cores(x) for x in halos])
    rounds = in_order(fetch_weights(shard))
    taps = build_taps(two, own, other, lanes)
    rounds2 = [swap_cores(r) for r in rounds]
    keep, send, res_keep, res_send = forward(two, rounds, taps, current_bias[None], threshold[None])
    arrived = swap_cores(send)
    res_arrived = swap_cores(res_send)
    (partial,) = backward(two, rounds, keep, cot)
    input_grad, residual = backward(two, rounds2, arrived, partial, (res_keep, res_arrived))
    return residual[None], input_grad[None]


def solution(mesh):
    return jax.shard_map(
        on_device,
        mesh=mesh,
        in_specs=(
            P(("groups", "dp"), "tm", "rows", None, None),
            P(("groups", "dp"), "tm", "rows", None, None),
            P(None, None, None, "dp"),
            P(None, None, None, "dp"),
            P(),
            P(),
        ),
        out_specs=(
            P(("groups", "dp"), "tm", "rows", None, None),
            P(("groups", "dp"), "tm", "rows", None, None),
        ),
        check_vma=False,
    )
```

```python
import functools

import jax
import jax.numpy as jnp
from jax import lax
from jax.experimental import pallas as pl
from jax.experimental.pallas import tpu as pltpu
from jax.sharding import PartitionSpec as P

MX_BLOCK = 32
TAPS = 3
F32 = jnp.float32
BF16 = jnp.bfloat16
VMEM_SPEC = pl.BlockSpec(memory_space=pltpu.VMEM)
ANY_SPEC = pl.BlockSpec(memory_space=pl.ANY)
QUARTERS = 4


def call(body, out_shape, in_specs, mib, name, scratch=(), grid=(), out_specs=None):
    return pl.pallas_call(
        body,
        out_shape=out_shape,
        grid=grid,
        in_specs=in_specs,
        out_specs=out_specs or jax.tree.map(lambda _: VMEM_SPEC, out_shape),
        scratch_shapes=list(scratch),
        compiler_params=pltpu.CompilerParams(vmem_limit_bytes=mib << 20),
        name=name,
    )


def shape(dims, dtype=BF16):
    return jax.ShapeDtypeStruct(dims, dtype)


def dot(a, b, dims):
    return lax.dot_general(a, b, (dims, ((), ())), preferred_element_type=F32)


def quarter_here():
    return lax.axis_index("groups") * 2 + lax.rem(lax.axis_index("rows"), 2)


def prepare_kernel(two, codes_ref, exps_ref, spikes_ref, cot_ref, *refs):
    if two:
        w_ref, wq_ref, wd_ref, halo_ref, sems = refs
        halos = [(halo_ref, 1 - lax.axis_index("rows"))]
    else:
        w_ref, wq_ref, wd_ref, head_ref, tail_ref, sems = refs
        halos = [(head_ref, 0), (tail_ref, 1)]
    steps, rows = spikes_ref.shape[:2]
    copies = []
    for n, (ref, end) in enumerate(halos):
        for t in range(steps):
            s = spikes_ref.at[t, pl.ds(end * (rows - 2), 2)]
            c = cot_ref.at[t, pl.ds(end * (rows - 1), 1)]
            copies.append(pltpu.make_async_copy(s, ref.at[t, pl.ds(0, 2)], sems.at[len(copies)]))
            copies.append(pltpu.make_async_copy(c, ref.at[t, pl.ds(2, 1)], sems.at[len(copies)]))
    for copy in copies:
        copy.start()
    outs, ins = codes_ref.shape[2:]
    blocks = exps_ref.shape[1]
    width = w_ref.shape[2]
    spread = lax.broadcasted_iota(jnp.int32, (blocks, ins), 1) // MX_BLOCK
    spread = (spread == lax.broadcasted_iota(jnp.int32, (blocks, ins), 0)).astype(F32).astype(BF16)
    for dy in range(TAPS):
        parts = []
        for dx in range(TAPS):
            scale = 1.0 / lax.shift_left(jnp.int32(1), -exps_ref[dy, :, dx, :]).astype(F32)
            scale = dot(scale.astype(BF16), spread, ((0,), (0,)))
            parts.append(codes_ref[dy, dx].astype(F32) * scale)
        parts.append(jnp.zeros((outs, QUARTERS * width - TAPS * ins), F32))
        tap = jnp.concatenate(parts, axis=1).astype(BF16)
        for q in range(QUARTERS):
            w_ref[q, dy * outs : (dy + 1) * outs, :] = tap[:, q * width : (q + 1) * width]
    q = quarter_here()
    wq_ref[...] = w_ref[q]
    wd_ref[...] = w_ref[QUARTERS - 1 - q]
    for copy in copies:
        copy.wait()


def prepare(two, weight_codes, block_exponents, spikes, cot):
    outs = weight_codes.shape[3]
    steps, rows, cols, ch = spikes.shape
    width = -(-TAPS * ch // (QUARTERS * 128)) * 128
    n_halo = 1 if two else 2
    w = shape((TAPS * outs, width))
    out = (shape((QUARTERS, TAPS * outs, width)), w, w) + (shape((steps, 3, cols, ch)),) * n_halo
    return call(
        functools.partial(prepare_kernel, two),
        out,
        [VMEM_SPEC] * 2 + [ANY_SPEC] * 2,
        16,
        "prepare",
        [pltpu.SemaphoreType.DMA((2 * steps * n_halo,))],
    )(weight_codes.transpose(0, 1, 3, 2), block_exponents.transpose(0, 2, 1, 3), spikes, cot)


def put_taps(x_ref, x, s, t):
    cols, ch = x.shape
    edge = lax.broadcasted_iota(jnp.int32, (cols, 1), 0)
    before = jnp.where(edge == 0, 0.0, pltpu.roll(x, 1, 0))
    after = jnp.where(edge == cols - 1, 0.0, pltpu.roll(x, cols - 1, 0))
    pad = jnp.zeros((cols, x_ref.shape[2] - TAPS * ch), F32)
    taps = jnp.concatenate([before, x, after, pad], axis=1)
    x_ref[s, pl.ds(pl.multiple_of(t * cols, cols), cols), :] = taps.astype(BF16)


def half_of(x):
    half = x.shape[-1] // 2
    return jnp.where(lax.axis_index("tm") == 0, x[:, :half], x[:, half:])


def taps_kernel(spikes_ref, spikes2_ref, cot_ref, cot2_ref, x_ref, s_ref, c_ref):
    steps, rows = spikes_ref.shape[:2]
    for which, (s_in, c_in) in enumerate(((spikes_ref, cot_ref), (spikes2_ref, cot2_ref))):

        def body(n, carry, s_in=s_in, c_in=c_in, which=which):
            t, h = n // rows, n % rows
            x = s_in[t, h].astype(F32)
            put_taps(x_ref, x, h, which * steps + t)
            s_ref[h, which * steps + t] = half_of(x).astype(BF16)
            c_ref[h, which * steps + t] = half_of(c_in[t, h].astype(F32)).astype(BF16)
            return carry

        lax.fori_loop(0, steps * rows, body, 0)


def build_taps(spikes, cot, spikes2, cot2, lanes):
    steps, rows, cols, ch = spikes.shape
    half = shape((rows, 2 * steps, cols, ch // 2))
    out = (shape((rows, 2 * steps * cols, lanes)), half, half)
    return call(taps_kernel, out, [VMEM_SPEC] * 4, 16, "taps")(spikes, spikes2, cot, cot2)


def halo_taps_kernel(halo_ref, halo2_ref, x_ref, c_ref):
    steps = halo_ref.shape[0]
    for which, ref in enumerate((halo_ref, halo2_ref)):

        def body(t, carry, ref=ref, which=which):
            for k in range(2):
                put_taps(x_ref, ref[t, k].astype(F32), k, which * steps + t)
            c_ref[which * steps + t] = half_of(ref[t, 2].astype(F32)).astype(BF16)
            return carry

        lax.fori_loop(0, steps, body, 0)


def build_halo_taps(halo, halo2, lanes):
    steps, _, cols, ch = halo.shape
    out = (shape((2, 2 * steps * cols, lanes)), shape((2 * steps, cols, ch // 2)))
    return call(halo_taps_kernel, out, [VMEM_SPEC] * 2, 16, "halo_taps")(halo, halo2)


def split_half(half):
    main = half // 128 * 128
    return main, half - main, TAPS * main + -(-TAPS * (half - main) // 128) * 128


def join_kernel(w_ref, *refs):
    rounds, out_ref = (refs[:QUARTERS], refs[QUARTERS : 2 * QUARTERS]), refs[-1]
    outs = w_ref.shape[1] // TAPS
    width = w_ref.shape[2]
    main, tail, _ = split_half(2 * outs)
    z, core, q = lax.axis_index("dp"), lax.axis_index("tm"), quarter_here()
    place = lax.rem(z, 2)
    own = core == z // 2

    def put(part, lane, pos):
        at = pl.ds(pl.multiple_of(lane * width, width), width)
        for dy in range(TAPS):
            for o in range(0, outs, 16):
                c = pos * outs + o
                to = dy * main + c if c < main else TAPS * main + dy * tail + c - main
                out_ref[to : to + 16, at] = part[dy * outs + o : dy * outs + o + 16, :]

    def put_round(k, pos):
        lanes_of = (q, QUARTERS - 1 - q, jnp.bitwise_xor(q, 1), jnp.bitwise_xor(q, 2))
        if k == 1:
            for part, lane in zip(rounds[1], lanes_of):
                put(part, lane, pos)
            return

        @pl.when(own)
        def _():
            for n in range(QUARTERS):
                put(w_ref[n], n, pos)

        @pl.when(jnp.logical_not(own))
        def _():
            for part, lane in zip(rounds[0], lanes_of):
                put(part, lane, pos)

    for even in range(2):

        @pl.when(place == even)
        def _():
            put_round(0, even)
            put_round(1, 1 - even)

    rest = out_ref.shape[0] - TAPS * 2 * outs
    out_ref[TAPS * 2 * outs :, :] = jnp.zeros((rest, out_ref.shape[1]), BF16)


def fetch_weights(w, wq, wd):
    count = lax.axis_size("dp")
    n_rows = lax.axis_size("rows")
    h = count // 2
    outs = w.shape[1] // TAPS
    lanes = QUARTERS * w.shape[2]

    def pairs(k):
        todo = []
        for z in range(count):
            for c in range(2):
                s = c * h + (z + k) % h
                todo.append((s * 2 + z // h, z * 2 + c))
        return todo

    main, tail, padded = split_half(h * outs)
    if h == 2 and outs % 16 == 0 and n_rows % 2 == 0 and lax.axis_size("groups") == 2:
        moved = [[(a, b) for a, b in pairs(k) if a != b] for k in range(h)]
        first = [lax.ppermute(wq, ("dp", "tm"), moved[k]) for k in range(h)]
        last = [lax.ppermute(wd, ("dp", "tm"), moved[k]) for k in range(h)]
        args = []
        for k in range(h):
            takes = [b for _, b in moved[k]]
            rows = [(d * n_rows + r, d * n_rows + (r ^ 1)) for d in takes for r in range(n_rows)]
            groups = [(g * 2 * count + d, (1 - g) * 2 * count + d) for d in takes for g in range(2)]
            x = lax.ppermute(first[k], ("dp", "tm", "rows"), rows)
            y = lax.ppermute(first[k], ("groups", "dp", "tm"), groups)
            args += [first[k], last[k], x, y]
        return call(join_kernel, shape((padded, lanes)), [VMEM_SPEC] * 9, 8, "join")(w, *args)
    w = w.reshape(QUARTERS, TAPS, outs, -1).transpose(1, 2, 0, 3).reshape(TAPS, outs, lanes)
    stack = jnp.stack([lax.ppermute(w, ("dp", "tm"), pairs(k)) for k in range(h)], axis=1)
    stack = jnp.roll(stack, lax.axis_index("dp") % h, axis=1).reshape(TAPS, h * outs, lanes)
    rest = jnp.zeros((padded - TAPS * h * outs, lanes), BF16)
    return jnp.concatenate([stack[:, :main].reshape(-1, lanes), stack[:, main:].reshape(-1, lanes), rest])


def forward_kernel(two, w_ref, x_ref, s_ref, c_ref, *refs):
    if two:
        halos = [refs[:2]]
    else:
        halos = [refs[:2], refs[2:4]]
    bias_ref, thr_ref, gk_ref, gs_ref, rk_ref, rs_ref, p_ref = refs[2 * len(halos) :]
    core, row = lax.axis_index("tm"), lax.axis_index("rows")
    rows, times, cols, half = s_ref.shape
    lanes = x_ref.shape[2]
    steps = times // 2
    main, tail, _ = split_half(half)
    chunk = 16

    def half_row(ref):
        return jnp.where(core == 0, ref[:, :half], ref[:, half:])

    thr = half_row(thr_ref)
    shift = half_row(bias_ref) - thr
    at_of = [lax.rem(core + part, 2) * steps + tl for part in range(2) for tl in range(steps)]

    def currents(x, strip):
        p = dot(x.reshape(-1, lanes), w_ref[...], ((1,), (1,)))
        p_ref[pl.ds(strip, 2)] = p.reshape(2, times * cols, -1)

    def scan(strip, cot, spike, g, h, keep=None):
        for w0 in range(0, cols, chunk):
            for lo, width, first in ((0, main, 0), (main, tail, TAPS * main)):
                th = thr[:, lo : lo + width]
                half_th = 0.5 * th
                sh = shift[:, lo : lo + width]
                state = jnp.zeros((chunk, width), F32)
                tanhs = []
                for t in range(times):
                    at = pl.ds(pl.multiple_of(at_of[t] * cols + w0, chunk), chunk)
                    now = sh
                    for dy in range(TAPS):
                        now = now + p_ref[strip + dy, at, first + dy * width : first + (dy + 1) * width]
                    y = state + now
                    tanh = jnp.tanh(y)
                    state = (y + half_th) - half_th * tanh
                    tanhs.append(tanh)
                adjoint = jnp.zeros((chunk, width), F32)
                grads, res = [None] * times, [None] * times
                for t in reversed(range(times)):
                    here = slice(w0, w0 + chunk), slice(lo, lo + width)
                    slope = 0.5 - 0.5 * (tanhs[t] * tanhs[t])
                    up = cot(at_of[t], here).astype(F32)
                    adjoint = adjoint + slope * (up - th * adjoint)
                    out = adjoint if keep is None else adjoint * keep
                    grads[t] = out.astype(BF16)
                    if h is not None:
                        fired = 0.5 + 0.5 * tanhs[t]
                        res[t] = (fired + spike(at_of[t], here).astype(F32)).astype(BF16)
                mine = core == 0
                for tl in range(steps):
                    a, b = grads[tl], grads[steps + tl]
                    gk_ref[tl, g, w0 : w0 + chunk, lo : lo + width] = jnp.where(mine, a, b)
                    gs_ref[tl, g, w0 : w0 + chunk, lo : lo + width] = jnp.where(mine, b, a)
                    if h is not None:
                        a, b = res[tl], res[steps + tl]
                        rk_ref[tl, h, w0 : w0 + chunk, lo : lo + width] = jnp.where(mine, a, b)
                        rs_ref[tl, h, w0 : w0 + chunk, lo : lo + width] = jnp.where(mine, b, a)

    def scan_own(h, strip):
        scan(
            strip,
            lambda at, here: c_ref[h, at, here[0], here[1]],
            lambda at, here: s_ref[h, at, here[0], here[1]],
            h + 1,
            h,
        )

    def scan_halo(n, strip, g, keep=None):
        scan(strip, lambda at, here: halos[n][1][at, here[0], here[1]], None, g, None, keep)

    if two:
        flip = row == 1
        edge_strip = jnp.where(flip, rows + 2, 0)
        edge = jnp.where(flip, rows + 1, 0)
        p_ref[edge_strip] = jnp.zeros(p_ref.shape[1:], F32)
        for ref in (gk_ref, gs_ref):
            for tl in range(steps):
                ref[tl, edge] = jnp.zeros((cols, half), BF16)

        def scan_at(j):
            if j == rows:
                scan_halo(0, jnp.where(flip, 0, rows), jnp.where(flip, 0, rows + 1))
            elif 0 <= j < rows:
                h = jnp.where(flip, rows - 1 - j, j)
                scan_own(h, jnp.where(flip, h + 1, h))

        done = 0
        for i in range(rows // 2 + 1):
            if i < rows // 2:
                h = jnp.where(flip, rows - 2 - 2 * i, 2 * i)
                currents(x_ref[pl.ds(h, 2)], jnp.where(flip, h + 2, h + 1))
            else:
                currents(halos[0][0][...], jnp.where(flip, 0, rows + 1))
            while done <= 2 * i - 2:
                scan_at(done)
                done += 1
        while done <= rows:
            scan_at(done)
            done += 1
    else:
        last = lax.axis_size("rows") - 1
        currents(halos[0][0][...], 0)
        currents(halos[1][0][...], rows + 2)

        def pair(i, carry):
            currents(x_ref[pl.ds(2 * i, 2)], 2 * i + 2)
            return carry

        lax.fori_loop(0, rows // 2, pair, 0)

        def one(h, carry):
            scan_own(h, h + 1)
            return carry

        lax.fori_loop(0, rows, one, 0)
        scan_halo(0, 0, 0, jnp.where(row == 0, 0.0, 1.0))
        scan_halo(1, rows + 1, rows + 1, jnp.where(row == last, 0.0, 1.0))


def forward(two, weights, taps, halo_taps, bias, thr):
    x, s, c = taps
    rows, times, cols, half = s.shape
    steps = times // 2
    args = [weights, x, s, c] + [a for pair in halo_taps for a in pair] + [bias, thr]
    grad = shape((steps, rows + 2, cols, half))
    res = shape((steps, rows, cols, half))
    return call(
        functools.partial(forward_kernel, two),
        (grad, grad, res, res),
        [VMEM_SPEC] * len(args),
        16,
        "forward",
        [pltpu.VMEM((rows + (3 if two else 4), times * cols, weights.shape[0]), F32)],
    )(*args)


def rows_of_grads(g_ref, t, h0, count):
    cols, half = g_ref.shape[2:]
    main, tail, padded = split_half(half)
    taps = [g_ref[t, pl.ds(h0 + 2 - dy, count)].reshape(count * cols, half) for dy in range(TAPS)]
    rest = jnp.zeros((count * cols, padded - TAPS * half), BF16)
    return jnp.concatenate([x[:, :main] for x in taps] + [x[:, main:] for x in taps] + [rest], axis=1)


def backward_own_kernel(w_ref, g_ref, y_ref):
    steps, rows2 = g_ref.shape[:2]
    rows = rows2 - 2
    for t in range(steps):
        grads = rows_of_grads(g_ref, t, 0, rows)
        y_ref[t] = dot(grads, w_ref[...], ((1,), (0,)))


def backward_own(weights, grads):
    steps, rows2, cols, _ = grads.shape
    out = shape((steps, (rows2 - 2) * cols, weights.shape[1]), F32)
    return call(backward_own_kernel, out, [VMEM_SPEC] * 2, 12, "backward_own")(weights, grads)


def backward_kernel(w_ref, g_ref, y_ref, cot_ref, rk_ref, rs_ref, out_ref, res_ref):
    t = pl.program_id(0)
    _, rows, cols, ch = cot_ref.shape
    core = lax.axis_index("tm")
    edge = lax.broadcasted_iota(jnp.int32, (1, cols, 1), 1)
    block = 4
    for h0 in range(0, rows, block):
        total = dot(rows_of_grads(g_ref, t, h0, block), w_ref[...], ((1,), (0,)))
        total = (total + y_ref[t, h0 * cols : (h0 + block) * cols, :]).reshape(block, cols, -1)
        left, mid, right = (total[:, :, k * ch : (k + 1) * ch] for k in range(TAPS))
        left = jnp.where(edge == cols - 1, 0.0, pltpu.roll(left, cols - 1, 1))
        right = jnp.where(edge == 0, 0.0, pltpu.roll(right, 1, 1))
        out_ref[0, h0 : h0 + block] = cot_ref[t, h0 : h0 + block].astype(F32) + (left + mid + right)
        a = rk_ref[t, h0 : h0 + block].astype(F32)
        b = rs_ref[t, h0 : h0 + block].astype(F32)
        both = jnp.concatenate([jnp.where(core == 0, a, b), jnp.where(core == 0, b, a)], axis=2)
        res_ref[0, h0 : h0 + block] = both.astype(BF16)


def backward(weights, grads, y, cot, res_keep, res_arrived):
    block = pl.BlockSpec((1,) + cot.shape[1:], lambda t: (t, 0, 0, 0))
    return call(
        backward_kernel,
        (shape(cot.shape, F32), shape(cot.shape)),
        [VMEM_SPEC] * 6,
        16,
        "backward",
        grid=(cot.shape[0],),
        out_specs=(block, block),
    )(weights, grads, y, cot, res_keep, res_arrived)


def swap_cores(x):
    return lax.ppermute(x, "tm", [(0, 1), (1, 0)])


def fetch_halos(two, halos):
    if two:
        return [lax.ppermute(halos[0], "rows", [(0, 1), (1, 0)])]
    count = lax.axis_size("rows")
    head, tail = halos
    return [
        lax.ppermute(tail, "rows", [(i, i + 1) for i in range(count - 1)]),
        lax.ppermute(head, "rows", [(i + 1, i) for i in range(count - 1)]),
    ]


def on_device(spikes, cotangent, weight_codes, block_exponents, current_bias, threshold):
    two = lax.axis_size("rows") == 2
    spikes, cot = spikes[0], cotangent[0]
    w, wq, wd, *halos = prepare(two, weight_codes, block_exponents, spikes, cot)
    lanes = QUARTERS * w.shape[2]
    halos = fetch_halos(two, halos)
    weights = fetch_weights(w, wq, wd)
    taps = build_taps(spikes, cot, swap_cores(spikes), swap_cores(cot), lanes)
    halo_taps = [build_halo_taps(x, swap_cores(x), lanes) for x in halos]
    weights2 = swap_cores(weights)
    keep, send, res_keep, res_send = forward(two, weights, taps, halo_taps, current_bias[None], threshold[None])
    arrived = swap_cores(send)
    res_arrived = swap_cores(res_send)
    y = backward_own(weights, keep)
    input_grad, residual = backward(weights2, arrived, y, cot, res_keep, res_arrived)
    return residual[None], input_grad[None]


def solution(mesh):
    return jax.shard_map(
        on_device,
        mesh=mesh,
        in_specs=(
            P(("groups", "dp"), "tm", "rows", None, None),
            P(("groups", "dp"), "tm", "rows", None, None),
            P(None, None, None, "dp"),
            P(None, None, None, "dp"),
            P(),
            P(),
        ),
        out_specs=(
            P(("groups", "dp"), "tm", "rows", None, None),
            P(("groups", "dp"), "tm", "rows", None, None),
        ),
        check_vma=False,
    )
```

```python
import functools

import jax
import jax.numpy as jnp
from jax import lax
from jax.experimental import pallas as pl
from jax.experimental.pallas import tpu as pltpu
from jax.sharding import PartitionSpec as P

MX_BLOCK = 32
TAPS = 3
F32 = jnp.float32
BF16 = jnp.bfloat16
VMEM_SPEC = pl.BlockSpec(memory_space=pltpu.VMEM)
HBM_SPEC = pl.BlockSpec(memory_space=pltpu.HBM)
QUARTERS = 4


def call(body, out_shape, in_specs, mib, name, scratch=(), grid=(), out_specs=None, cost=0):
    return pl.pallas_call(
        body,
        out_shape=out_shape,
        grid=grid,
        in_specs=in_specs,
        out_specs=out_specs or jax.tree.map(lambda _: VMEM_SPEC, out_shape),
        scratch_shapes=list(scratch),
        compiler_params=pltpu.CompilerParams(vmem_limit_bytes=mib << 20),
        cost_estimate=pl.CostEstimate(flops=0, transcendentals=0, bytes_accessed=cost) if cost else None,
        name=name,
    )


def in_hbm(x):
    return pltpu.with_memory_space_constraint(x, pltpu.HBM)


def shape(dims, dtype=BF16):
    return jax.ShapeDtypeStruct(dims, dtype)


def dot(a, b, dims):
    return lax.dot_general(a, b, (dims, ((), ())), preferred_element_type=F32)


def quarter_here():
    return lax.axis_index("groups") * 2 + lax.rem(lax.axis_index("rows"), 2)


def prepare_kernel(two, codes_hbm, exps_hbm, spikes_ref, cot_ref, *refs):
    w_ref, wq_ref, wd_ref = refs[:3]
    halo_refs, (codes_ref, exps_ref, sems, code_sems) = refs[3:-4], refs[-4:]
    if two:
        halos = [(halo_refs[0], 1 - lax.axis_index("rows"))]
    else:
        halos = [(halo_refs[0], 0), (halo_refs[1], 1)]
    steps, rows = spikes_ref.shape[:2]
    scales = pltpu.make_async_copy(exps_hbm, exps_ref, code_sems.at[TAPS])
    codes = [pltpu.make_async_copy(codes_hbm.at[dy], codes_ref.at[dy], code_sems.at[dy]) for dy in range(TAPS)]
    scales.start()
    for copy in codes:
        copy.start()
    copies = []
    for n, (ref, end) in enumerate(halos):
        for t in range(steps):
            s = spikes_ref.at[t, pl.ds(end * (rows - 2), 2)]
            c = cot_ref.at[t, pl.ds(end * (rows - 1), 1)]
            copies.append(pltpu.make_async_copy(s, ref.at[t, pl.ds(0, 2)], sems.at[len(copies)]))
            copies.append(pltpu.make_async_copy(c, ref.at[t, pl.ds(2, 1)], sems.at[len(copies)]))
    for copy in copies:
        copy.start()
    outs, ins = codes_ref.shape[2:]
    blocks = exps_ref.shape[1]
    width = w_ref.shape[2]
    spread = lax.broadcasted_iota(jnp.int32, (blocks, ins), 1) // MX_BLOCK
    spread = (spread == lax.broadcasted_iota(jnp.int32, (blocks, ins), 0)).astype(F32).astype(BF16)
    scales.wait()
    for dy in range(TAPS):
        codes[dy].wait()
        parts = []
        for dx in range(TAPS):
            scale = 1.0 / lax.shift_left(jnp.int32(1), -exps_ref[dy, :, dx, :]).astype(F32)
            scale = dot(scale.astype(BF16), spread, ((0,), (0,)))
            parts.append(codes_ref[dy, dx].astype(F32) * scale)
        parts.append(jnp.zeros((outs, QUARTERS * width - TAPS * ins), F32))
        tap = jnp.concatenate(parts, axis=1).astype(BF16)
        for q in range(QUARTERS):
            w_ref[q, dy * outs : (dy + 1) * outs, :] = tap[:, q * width : (q + 1) * width]
    q = quarter_here()
    wq_ref[...] = w_ref[q]
    wd_ref[...] = w_ref[QUARTERS - 1 - q]
    for copy in copies:
        copy.wait()


def prepare(two, weight_codes, block_exponents, spikes, cot):
    outs = weight_codes.shape[3]
    steps, rows, cols, ch = spikes.shape
    width = -(-TAPS * ch // (QUARTERS * 128)) * 128
    n_halo = 1 if two else 2
    w = shape((TAPS * outs, width))
    out = (shape((QUARTERS, TAPS * outs, width)), w, w) + (shape((steps, 3, cols, ch)),) * n_halo
    return call(
        functools.partial(prepare_kernel, two),
        out,
        [HBM_SPEC] * 4,
        16,
        "prepare",
        [
            pltpu.VMEM((TAPS, TAPS, outs, ch), jnp.int32),
            pltpu.VMEM((TAPS, block_exponents.shape[2], TAPS, outs), jnp.int32),
            pltpu.SemaphoreType.DMA((2 * steps * n_halo,)),
            pltpu.SemaphoreType.DMA((TAPS + 1,)),
        ],
        cost=2 << 20,
    )(*map(in_hbm, (weight_codes.transpose(0, 1, 3, 2), block_exponents.transpose(0, 2, 1, 3), spikes, cot)))


def put_taps(x_ref, x, s, t):
    cols, ch = x.shape
    edge = lax.broadcasted_iota(jnp.int32, (cols, 1), 0)
    before = jnp.where(edge == 0, 0.0, pltpu.roll(x, 1, 0))
    after = jnp.where(edge == cols - 1, 0.0, pltpu.roll(x, cols - 1, 0))
    pad = jnp.zeros((cols, x_ref.shape[2] - TAPS * ch), F32)
    taps = jnp.concatenate([before, x, after, pad], axis=1)
    x_ref[s, pl.ds(pl.multiple_of(t * cols, cols), cols), :] = taps.astype(BF16)


def half_of(x):
    half = x.shape[-1] // 2
    return jnp.where(lax.axis_index("tm") == 0, x[:, :half], x[:, half:])


def taps_kernel(spikes_ref, spikes2_ref, cot_ref, cot2_ref, x_ref, s_ref, c_ref):
    steps, rows = spikes_ref.shape[:2]
    for which, (s_in, c_in) in enumerate(((spikes_ref, cot_ref), (spikes2_ref, cot2_ref))):

        def body(n, carry, s_in=s_in, c_in=c_in, which=which):
            t, h = n // rows, n % rows
            x = s_in[t, h].astype(F32)
            put_taps(x_ref, x, h, which * steps + t)
            s_ref[h, which * steps + t] = half_of(x).astype(BF16)
            c_ref[h, which * steps + t] = half_of(c_in[t, h].astype(F32)).astype(BF16)
            return carry

        lax.fori_loop(0, steps * rows, body, 0)


def build_taps(spikes, cot, spikes2, cot2, lanes):
    steps, rows, cols, ch = spikes.shape
    half = shape((rows, 2 * steps, cols, ch // 2))
    out = (shape((rows, 2 * steps * cols, lanes)), half, half)
    return call(taps_kernel, out, [VMEM_SPEC] * 4, 16, "taps", cost=18 << 20)(spikes, spikes2, cot, cot2)


def halo_taps_kernel(halo_ref, halo2_ref, x_ref, c_ref):
    steps = halo_ref.shape[0]
    for which, ref in enumerate((halo_ref, halo2_ref)):

        def body(t, carry, ref=ref, which=which):
            for k in range(2):
                put_taps(x_ref, ref[t, k].astype(F32), k, which * steps + t)
            c_ref[which * steps + t] = half_of(ref[t, 2].astype(F32)).astype(BF16)
            return carry

        lax.fori_loop(0, steps, body, 0)


def build_halo_taps(halo, halo2, lanes):
    steps, _, cols, ch = halo.shape
    out = (shape((2, 2 * steps * cols, lanes)), shape((2 * steps, cols, ch // 2)))
    return call(halo_taps_kernel, out, [VMEM_SPEC] * 2, 16, "halo_taps", cost=2 << 20)(halo, halo2)


def split_half(half):
    main = half // 128 * 128
    return main, half - main, TAPS * main + -(-TAPS * (half - main) // 128) * 128


def join_kernel(w_ref, *refs):
    first, last, (x_ref, y_ref), out_ref = refs[:2], refs[2:4], refs[4:6], refs[-1]
    size = w_ref.shape[1]
    rounds = [(first[k], last[k], x_ref.at[k * size : (k + 1) * size], y_ref.at[k * size : (k + 1) * size]) for k in range(2)]
    outs = w_ref.shape[1] // TAPS
    width = w_ref.shape[2]
    main, tail, _ = split_half(2 * outs)
    z, core, q = lax.axis_index("dp"), lax.axis_index("tm"), quarter_here()
    place = lax.rem(z, 2)
    own = core == z // 2

    def put(part, lane, pos):
        at = pl.ds(pl.multiple_of(lane * width, width), width)
        for dy in range(TAPS):
            for o in range(0, outs, 16):
                c = pos * outs + o
                to = dy * main + c if c < main else TAPS * main + dy * tail + c - main
                out_ref[to : to + 16, at] = part[dy * outs + o : dy * outs + o + 16, :]

    def put_round(k, pos):
        lanes_of = (q, QUARTERS - 1 - q, jnp.bitwise_xor(q, 1), jnp.bitwise_xor(q, 2))
        if k == 1:
            for part, lane in zip(rounds[1], lanes_of):
                put(part, lane, pos)
            return

        @pl.when(own)
        def _():
            for n in range(QUARTERS):
                put(w_ref[n], n, pos)

        @pl.when(jnp.logical_not(own))
        def _():
            for part, lane in zip(rounds[0], lanes_of):
                put(part, lane, pos)

    for even in range(2):

        @pl.when(place == even)
        def _():
            put_round(0, even)
            put_round(1, 1 - even)

    rest = out_ref.shape[0] - TAPS * 2 * outs
    out_ref[TAPS * 2 * outs :, :] = jnp.zeros((rest, out_ref.shape[1]), BF16)


def fetch_weights(w, wq, wd, after):
    count = lax.axis_size("dp")
    n_rows = lax.axis_size("rows")
    h = count // 2
    outs = w.shape[1] // TAPS
    lanes = QUARTERS * w.shape[2]

    def pairs(k):
        todo = []
        for z in range(count):
            for c in range(2):
                s = c * h + (z + k) % h
                todo.append((s * 2 + z // h, z * 2 + c))
        return todo

    main, tail, padded = split_half(h * outs)
    if h == 2 and outs % 16 == 0 and n_rows % 2 == 0 and lax.axis_size("groups") == 2:
        moved = [[(a, b) for a, b in pairs(k) if a != b] for k in range(h)]
        first = [lax.ppermute(wq, ("dp", "tm"), moved[k]) for k in range(h)]
        last = [lax.ppermute(wd, ("dp", "tm"), moved[k]) for k in range(h)]
        both, after = lax.optimization_barrier((first, after))
        both = jnp.concatenate(both)
        x = lax.ppermute(both, "rows", [(r, r ^ 1) for r in range(n_rows)])
        y = lax.ppermute(both, "groups", [(0, 1), (1, 0)])
        parts = first + last + [x, y]
        return lambda w: call(join_kernel, shape((padded, lanes)), [VMEM_SPEC] * 7, 8, "join")(w, *parts), after
    w = w.reshape(QUARTERS, TAPS, outs, -1).transpose(1, 2, 0, 3).reshape(TAPS, outs, lanes)
    stack = jnp.stack([lax.ppermute(w, ("dp", "tm"), pairs(k)) for k in range(h)], axis=1)
    stack = jnp.roll(stack, lax.axis_index("dp") % h, axis=1).reshape(TAPS, h * outs, lanes)
    rest = jnp.zeros((padded - TAPS * h * outs, lanes), BF16)
    joined = jnp.concatenate([stack[:, :main].reshape(-1, lanes), stack[:, main:].reshape(-1, lanes), rest])
    return lambda w: joined, after


def forward_kernel(two, w_ref, x_ref, s_ref, c_ref, *refs):
    if two:
        halos = [refs[:2]]
    else:
        halos = [refs[:2], refs[2:4]]
    bias_ref, thr_ref, gk_ref, gs_ref, rk_ref, rs_ref, p_ref = refs[2 * len(halos) :]
    core, row = lax.axis_index("tm"), lax.axis_index("rows")
    rows, times, cols, half = s_ref.shape
    lanes = x_ref.shape[2]
    steps = times // 2
    main, tail, _ = split_half(half)
    chunk = 16

    def half_row(ref):
        x = ref[...].reshape(1, 2 * half)
        return jnp.where(core == 0, x[:, :half], x[:, half:])

    thr = half_row(thr_ref)
    shift = half_row(bias_ref) - thr
    at_of = [lax.rem(core + part, 2) * steps + tl for part in range(2) for tl in range(steps)]

    def currents(x, strip):
        p = dot(x.reshape(-1, lanes), w_ref[...], ((1,), (1,)))
        p_ref[pl.ds(strip, 2)] = p.reshape(2, times * cols, -1)

    def scan(strip, cot, spike, g, h, keep=None):
        for w0 in range(0, cols, chunk):
            for lo, width, first in ((0, main, 0), (main, tail, TAPS * main)):
                th = thr[:, lo : lo + width]
                half_th = 0.5 * th
                sh = shift[:, lo : lo + width]
                state = jnp.zeros((chunk, width), F32)
                tanhs = []
                for t in range(times):
                    at = pl.ds(pl.multiple_of(at_of[t] * cols + w0, chunk), chunk)
                    now = sh
                    for dy in range(TAPS):
                        now = now + p_ref[strip + dy, at, first + dy * width : first + (dy + 1) * width]
                    y = state + now
                    tanh = jnp.tanh(y)
                    state = (y + half_th) - half_th * tanh
                    tanhs.append(tanh)
                adjoint = jnp.zeros((chunk, width), F32)
                grads, res = [None] * times, [None] * times
                for t in reversed(range(times)):
                    here = slice(w0, w0 + chunk), slice(lo, lo + width)
                    slope = 0.5 - 0.5 * (tanhs[t] * tanhs[t])
                    up = cot(at_of[t], here).astype(F32)
                    adjoint = adjoint + slope * (up - th * adjoint)
                    out = adjoint if keep is None else adjoint * keep
                    grads[t] = out.astype(BF16)
                    if h is not None:
                        fired = 0.5 + 0.5 * tanhs[t]
                        res[t] = (fired + spike(at_of[t], here).astype(F32)).astype(BF16)
                mine = core == 0
                for tl in range(steps):
                    a, b = grads[tl], grads[steps + tl]
                    gk_ref[tl, g, w0 : w0 + chunk, lo : lo + width] = jnp.where(mine, a, b)
                    gs_ref[tl, g, w0 : w0 + chunk, lo : lo + width] = jnp.where(mine, b, a)
                    if h is not None:
                        a, b = res[tl], res[steps + tl]
                        rk_ref[tl, h, w0 : w0 + chunk, lo : lo + width] = jnp.where(mine, a, b)
                        rs_ref[tl, h, w0 : w0 + chunk, lo : lo + width] = jnp.where(mine, b, a)

    def scan_own(h, strip):
        scan(
            strip,
            lambda at, here: c_ref[h, at, here[0], here[1]],
            lambda at, here: s_ref[h, at, here[0], here[1]],
            h + 1,
            h,
        )

    def scan_halo(n, strip, g, keep=None):
        scan(strip, lambda at, here: halos[n][1][at, here[0], here[1]], None, g, None, keep)

    if two:
        flip = row == 1
        edge_strip = jnp.where(flip, rows + 2, 0)
        edge = jnp.where(flip, rows + 1, 0)
        p_ref[edge_strip] = jnp.zeros(p_ref.shape[1:], F32)
        for ref in (gk_ref, gs_ref):
            for tl in range(steps):
                ref[tl, edge] = jnp.zeros((cols, half), BF16)

        def scan_at(j):
            if j == rows:
                scan_halo(0, jnp.where(flip, 0, rows), jnp.where(flip, 0, rows + 1))
            elif 0 <= j < rows:
                h = jnp.where(flip, rows - 1 - j, j)
                scan_own(h, jnp.where(flip, h + 1, h))

        done = 0
        for i in range(rows // 2 + 1):
            if i < rows // 2:
                h = jnp.where(flip, rows - 2 - 2 * i, 2 * i)
                currents(x_ref[pl.ds(h, 2)], jnp.where(flip, h + 2, h + 1))
            else:
                currents(halos[0][0][...], jnp.where(flip, 0, rows + 1))
            while done <= 2 * i - 2:
                scan_at(done)
                done += 1
        while done <= rows:
            scan_at(done)
            done += 1
    else:
        last = lax.axis_size("rows") - 1
        currents(halos[0][0][...], 0)
        currents(halos[1][0][...], rows + 2)

        def pair(i, carry):
            currents(x_ref[pl.ds(2 * i, 2)], 2 * i + 2)
            return carry

        lax.fori_loop(0, rows // 2, pair, 0)

        def one(h, carry):
            scan_own(h, h + 1)
            return carry

        lax.fori_loop(0, rows, one, 0)
        scan_halo(0, 0, 0, jnp.where(row == 0, 0.0, 1.0))
        scan_halo(1, rows + 1, rows + 1, jnp.where(row == last, 0.0, 1.0))


def forward(two, weights, taps, halo_taps, bias, thr):
    x, s, c = taps
    rows, times, cols, half = s.shape
    steps = times // 2
    args = [weights, x, s, c] + [a for pair in halo_taps for a in pair] + [bias, thr]
    grad = shape((steps, rows + 2, cols, half))
    res = shape((steps, rows, cols, half))
    return call(
        functools.partial(forward_kernel, two),
        (grad, grad, res, res),
        [VMEM_SPEC] * len(args),
        16,
        "forward",
        [pltpu.VMEM((rows + (3 if two else 4), times * cols, weights.shape[0]), F32)],
        cost=24 << 20,
    )(*args)


def rows_of_grads(g_ref, t, h0, count):
    cols, half = g_ref.shape[2:]
    main, tail, padded = split_half(half)
    taps = [g_ref[t, pl.ds(h0 + 2 - dy, count)].reshape(count * cols, half) for dy in range(TAPS)]
    rest = jnp.zeros((count * cols, padded - TAPS * half), BF16)
    return jnp.concatenate([x[:, :main] for x in taps] + [x[:, main:] for x in taps] + [rest], axis=1)


def backward_own_kernel(w_ref, g_ref, y_ref):
    steps, rows2 = g_ref.shape[:2]
    rows = rows2 - 2
    for t in range(steps):
        grads = rows_of_grads(g_ref, t, 0, rows)
        y_ref[t] = dot(grads, w_ref[...], ((1,), (0,)))


def backward_own(weights, grads):
    steps, rows2, cols, _ = grads.shape
    out = shape((steps, (rows2 - 2) * cols, weights.shape[1]), F32)
    return call(backward_own_kernel, out, [VMEM_SPEC] * 2, 12, "backward_own", cost=6 << 20)(weights, grads)


def backward_kernel(w_ref, g_ref, y_ref, cot_ref, rk_ref, rs_ref, out_ref, res_ref):
    t = pl.program_id(0)
    _, rows, cols, ch = cot_ref.shape
    core = lax.axis_index("tm")
    edge = lax.broadcasted_iota(jnp.int32, (1, cols, 1), 1)
    block = 4
    for h0 in range(0, rows, block):
        total = dot(rows_of_grads(g_ref, t, h0, block), w_ref[...], ((1,), (0,)))
        total = (total + y_ref[t, h0 * cols : (h0 + block) * cols, :]).reshape(block, cols, -1)
        left, mid, right = (total[:, :, k * ch : (k + 1) * ch] for k in range(TAPS))
        left = jnp.where(edge == cols - 1, 0.0, pltpu.roll(left, cols - 1, 1))
        right = jnp.where(edge == 0, 0.0, pltpu.roll(right, 1, 1))
        out_ref[0, h0 : h0 + block] = cot_ref[t, h0 : h0 + block].astype(F32) + (left + mid + right)
        a = rk_ref[t, h0 : h0 + block].astype(F32)
        b = rs_ref[t, h0 : h0 + block].astype(F32)
        both = jnp.concatenate([jnp.where(core == 0, a, b), jnp.where(core == 0, b, a)], axis=2)
        res_ref[0, h0 : h0 + block] = both.astype(BF16)


def backward(weights, grads, y, cot, res_keep, res_arrived):
    block = pl.BlockSpec((1,) + cot.shape[1:], lambda t: (t, 0, 0, 0))
    return call(
        backward_kernel,
        (shape(cot.shape, F32), shape(cot.shape)),
        [VMEM_SPEC] * 6,
        16,
        "backward",
        grid=(cot.shape[0],),
        out_specs=(block, block),
    )(weights, grads, y, cot, res_keep, res_arrived)


def swap_cores(x):
    return lax.ppermute(x, "tm", [(0, 1), (1, 0)])


def fetch_halos(two, halos):
    if two:
        return [lax.ppermute(halos[0], "rows", [(0, 1), (1, 0)])]
    count = lax.axis_size("rows")
    head, tail = halos
    return [
        lax.ppermute(tail, "rows", [(i, i + 1) for i in range(count - 1)]),
        lax.ppermute(head, "rows", [(i + 1, i) for i in range(count - 1)]),
    ]


def on_device(spikes, cotangent, weight_codes, block_exponents, current_bias, threshold):
    two = lax.axis_size("rows") == 2
    spikes, cot = spikes[0], cotangent[0]
    w, wq, wd, *halos = prepare(two, weight_codes, block_exponents, spikes, cot)
    lanes = QUARTERS * w.shape[2]
    halos = fetch_halos(two, halos)
    join, inputs = fetch_weights(w, wq, wd, (spikes, cot, swap_cores(spikes), swap_cores(cot)))
    taps, halos = lax.optimization_barrier((build_taps(*inputs, lanes), halos))
    halo_taps = [build_halo_taps(x, swap_cores(x), lanes) for x in halos]
    w, taps, halo_taps = lax.optimization_barrier((w, taps, halo_taps))
    weights = join(w)
    weights2 = swap_cores(weights)
    keep, send, res_keep, res_send = forward(two, weights, taps, halo_taps, current_bias, threshold)
    arrived = swap_cores(send)
    res_arrived = swap_cores(res_send)
    y = backward_own(weights, keep)
    input_grad, residual = backward(weights2, arrived, y, cot, res_keep, res_arrived)
    return residual[None], input_grad[None]


def solution(mesh):
    return jax.shard_map(
        on_device,
        mesh=mesh,
        in_specs=(
            P(("groups", "dp"), "tm", "rows", None, None),
            P(("groups", "dp"), "tm", "rows", None, None),
            P(None, None, None, "dp"),
            P(None, None, None, "dp"),
            P(),
            P(),
        ),
        out_specs=(
            P(("groups", "dp"), "tm", "rows", None, None),
            P(("groups", "dp"), "tm", "rows", None, None),
        ),
        check_vma=False,
    )
```

```python
import functools

import jax
import jax.numpy as jnp
from jax import lax
from jax.experimental import pallas as pl
from jax.experimental.pallas import tpu as pltpu
from jax.sharding import PartitionSpec as P

MX_BLOCK = 32
TAPS = 3
F32 = jnp.float32
BF16 = jnp.bfloat16
VMEM_SPEC = pl.BlockSpec(memory_space=pltpu.VMEM)
HBM_SPEC = pl.BlockSpec(memory_space=pltpu.HBM)
QUARTERS = 4


def call(body, out_shape, in_specs, mib, name, scratch=(), grid=(), out_specs=None, cost=0):
    return pl.pallas_call(
        body,
        out_shape=out_shape,
        grid=grid,
        in_specs=in_specs,
        out_specs=out_specs or jax.tree.map(lambda _: VMEM_SPEC, out_shape),
        scratch_shapes=list(scratch),
        compiler_params=pltpu.CompilerParams(vmem_limit_bytes=mib << 20),
        cost_estimate=pl.CostEstimate(flops=0, transcendentals=0, bytes_accessed=cost) if cost else None,
        name=name,
    )


def in_hbm(x):
    return pltpu.with_memory_space_constraint(x, pltpu.HBM)


def shape(dims, dtype=BF16):
    return jax.ShapeDtypeStruct(dims, dtype)


def dot(a, b, dims):
    return lax.dot_general(a, b, (dims, ((), ())), preferred_element_type=F32)


def quarter_here():
    return lax.axis_index("groups") * 2 + lax.rem(lax.axis_index("rows"), 2)


def prepare_kernel(two, codes_hbm, exps_hbm, spikes_ref, cot_ref, *refs):
    w_ref, wq_ref, wd_ref = refs[:3]
    halo_refs, (codes_ref, exps_ref, sems, code_sems) = refs[3:-4], refs[-4:]
    if two:
        halos = [(halo_refs[0], 1 - lax.axis_index("rows"))]
    else:
        halos = [(halo_refs[0], 0), (halo_refs[1], 1)]
    steps, rows = spikes_ref.shape[:2]
    scales = pltpu.make_async_copy(exps_hbm, exps_ref, code_sems.at[TAPS])
    codes = [pltpu.make_async_copy(codes_hbm.at[dy], codes_ref.at[dy], code_sems.at[dy]) for dy in range(TAPS)]
    scales.start()
    for copy in codes:
        copy.start()
    copies = []
    for n, (ref, end) in enumerate(halos):
        for t in range(steps):
            s = spikes_ref.at[t, pl.ds(end * (rows - 2), 2)]
            c = cot_ref.at[t, pl.ds(end * (rows - 1), 1)]
            copies.append(pltpu.make_async_copy(s, ref.at[t, pl.ds(0, 2)], sems.at[len(copies)]))
            copies.append(pltpu.make_async_copy(c, ref.at[t, pl.ds(2, 1)], sems.at[len(copies)]))
    for copy in copies:
        copy.start()
    outs, ins = codes_ref.shape[2:]
    blocks = exps_ref.shape[1]
    width = w_ref.shape[2]
    spread = lax.broadcasted_iota(jnp.int32, (blocks, ins), 1) // MX_BLOCK
    spread = (spread == lax.broadcasted_iota(jnp.int32, (blocks, ins), 0)).astype(F32).astype(BF16)
    scales.wait()
    for dy in range(TAPS):
        codes[dy].wait()
        parts = []
        for dx in range(TAPS):
            scale = 1.0 / lax.shift_left(jnp.int32(1), -exps_ref[dy, :, dx, :]).astype(F32)
            scale = dot(scale.astype(BF16), spread, ((0,), (0,)))
            parts.append(codes_ref[dy, dx].astype(F32) * scale)
        parts.append(jnp.zeros((outs, QUARTERS * width - TAPS * ins), F32))
        tap = jnp.concatenate(parts, axis=1).astype(BF16)
        for q in range(QUARTERS):
            w_ref[q, dy * outs : (dy + 1) * outs, :] = tap[:, q * width : (q + 1) * width]
    q = quarter_here()
    wq_ref[...] = w_ref[q]
    wd_ref[...] = w_ref[QUARTERS - 1 - q]
    for copy in copies:
        copy.wait()


def prepare(two, weight_codes, block_exponents, spikes, cot):
    outs = weight_codes.shape[3]
    steps, rows, cols, ch = spikes.shape
    width = -(-TAPS * ch // (QUARTERS * 128)) * 128
    n_halo = 1 if two else 2
    w = shape((TAPS * outs, width))
    out = (shape((QUARTERS, TAPS * outs, width)), w, w) + (shape((steps, 3, cols, ch)),) * n_halo
    return call(
        functools.partial(prepare_kernel, two),
        out,
        [HBM_SPEC] * 4,
        16,
        "prepare",
        [
            pltpu.VMEM((TAPS, TAPS, outs, ch), jnp.int32),
            pltpu.VMEM((TAPS, block_exponents.shape[2], TAPS, outs), jnp.int32),
            pltpu.SemaphoreType.DMA((2 * steps * n_halo,)),
            pltpu.SemaphoreType.DMA((TAPS + 1,)),
        ],
        cost=2 << 20,
    )(*map(in_hbm, (weight_codes.transpose(0, 1, 3, 2), block_exponents.transpose(0, 2, 1, 3), spikes, cot)))


def put_taps(x_ref, x, s, t):
    cols, ch = x.shape
    edge = lax.broadcasted_iota(jnp.int32, (cols, 1), 0)
    before = jnp.where(edge == 0, 0.0, pltpu.roll(x, 1, 0))
    after = jnp.where(edge == cols - 1, 0.0, pltpu.roll(x, cols - 1, 0))
    pad = jnp.zeros((cols, x_ref.shape[2] - TAPS * ch), F32)
    taps = jnp.concatenate([before, x, after, pad], axis=1)
    x_ref[s, pl.ds(pl.multiple_of(t * cols, cols), cols), :] = taps.astype(BF16)


def half_of(x):
    half = x.shape[-1] // 2
    return jnp.where(lax.axis_index("tm") == 0, x[:, :half], x[:, half:])


def taps_kernel(spikes_ref, spikes2_ref, cot_ref, cot2_ref, x_ref, s_ref, c_ref):
    steps, rows = spikes_ref.shape[:2]
    for which, (s_in, c_in) in enumerate(((spikes_ref, cot_ref), (spikes2_ref, cot2_ref))):

        def body(n, carry, s_in=s_in, c_in=c_in, which=which):
            t, h = n // rows, n % rows
            x = s_in[t, h].astype(F32)
            put_taps(x_ref, x, h, which * steps + t)
            s_ref[h, which * steps + t] = half_of(x).astype(BF16)
            c_ref[h, which * steps + t] = half_of(c_in[t, h].astype(F32)).astype(BF16)
            return carry

        lax.fori_loop(0, steps * rows, body, 0)


def build_taps(spikes, cot, spikes2, cot2, lanes):
    steps, rows, cols, ch = spikes.shape
    half = shape((rows, 2 * steps, cols, ch // 2))
    out = (shape((rows, 2 * steps * cols, lanes)), half, half)
    return call(taps_kernel, out, [VMEM_SPEC] * 4, 16, "taps", cost=18 << 20)(spikes, spikes2, cot, cot2)


def halo_taps_kernel(halo_ref, halo2_ref, x_ref, c_ref):
    steps = halo_ref.shape[0]
    for which, ref in enumerate((halo_ref, halo2_ref)):

        def body(t, carry, ref=ref, which=which):
            for k in range(2):
                put_taps(x_ref, ref[t, k].astype(F32), k, which * steps + t)
            c_ref[which * steps + t] = half_of(ref[t, 2].astype(F32)).astype(BF16)
            return carry

        lax.fori_loop(0, steps, body, 0)


def build_halo_taps(halo, halo2, lanes):
    steps, _, cols, ch = halo.shape
    out = (shape((2, 2 * steps * cols, lanes)), shape((2 * steps, cols, ch // 2)))
    return call(halo_taps_kernel, out, [VMEM_SPEC] * 2, 16, "halo_taps", cost=2 << 20)(halo, halo2)


def split_half(half):
    main = half // 128 * 128
    return main, half - main, TAPS * main + -(-TAPS * (half - main) // 128) * 128


def join_kernel(w_ref, *refs):
    first, last, (x_ref, y_ref), out_ref = refs[:2], refs[2:4], refs[4:6], refs[-1]
    size = w_ref.shape[1]
    rounds = [(first[k], last[k], x_ref.at[k * size : (k + 1) * size], y_ref.at[k * size : (k + 1) * size]) for k in range(2)]
    outs = w_ref.shape[1] // TAPS
    width = w_ref.shape[2]
    main, tail, _ = split_half(2 * outs)
    z, core, q = lax.axis_index("dp"), lax.axis_index("tm"), quarter_here()
    place = lax.rem(z, 2)
    own = core == z // 2

    def put(part, lane, pos):
        at = pl.ds(pl.multiple_of(lane * width, width), width)
        for dy in range(TAPS):
            for o in range(0, outs, 16):
                c = pos * outs + o
                to = dy * main + c if c < main else TAPS * main + dy * tail + c - main
                out_ref[to : to + 16, at] = part[dy * outs + o : dy * outs + o + 16, :]

    def put_round(k, pos):
        lanes_of = (q, QUARTERS - 1 - q, jnp.bitwise_xor(q, 1), jnp.bitwise_xor(q, 2))
        if k == 1:
            for part, lane in zip(rounds[1], lanes_of):
                put(part, lane, pos)
            return

        @pl.when(own)
        def _():
            for n in range(QUARTERS):
                put(w_ref[n], n, pos)

        @pl.when(jnp.logical_not(own))
        def _():
            for part, lane in zip(rounds[0], lanes_of):
                put(part, lane, pos)

    for even in range(2):

        @pl.when(place == even)
        def _():
            put_round(0, even)
            put_round(1, 1 - even)

    rest = out_ref.shape[0] - TAPS * 2 * outs
    out_ref[TAPS * 2 * outs :, :] = jnp.zeros((rest, out_ref.shape[1]), BF16)


def fetch_weights(w, wq, wd, after):
    count = lax.axis_size("dp")
    n_rows = lax.axis_size("rows")
    h = count // 2
    outs = w.shape[1] // TAPS
    lanes = QUARTERS * w.shape[2]

    def pairs(k):
        todo = []
        for z in range(count):
            for c in range(2):
                s = c * h + (z + k) % h
                todo.append((s * 2 + z // h, z * 2 + c))
        return todo

    main, tail, padded = split_half(h * outs)
    if h == 2 and outs % 16 == 0 and n_rows % 2 == 0 and lax.axis_size("groups") == 2:
        moved = [[(a, b) for a, b in pairs(k) if a != b] for k in range(h)]
        first = [lax.ppermute(wq, ("dp", "tm"), moved[k]) for k in range(h)]
        last = [lax.ppermute(wd, ("dp", "tm"), moved[k]) for k in range(h)]
        first, (taps, halos) = lax.optimization_barrier((first, (after[0], after[1])))
        both = jnp.concatenate(first)
        held, halos = lax.optimization_barrier((both, halos))
        after = taps, halos
        x = lax.ppermute(both, "rows", [(r, r ^ 1) for r in range(n_rows)])
        y = lax.ppermute(both, "groups", [(0, 1), (1, 0)])
        parts = first + last + [x, y]
        return lambda w: call(join_kernel, shape((padded, lanes)), [VMEM_SPEC] * 7, 8, "join")(w, *parts), after
    w = w.reshape(QUARTERS, TAPS, outs, -1).transpose(1, 2, 0, 3).reshape(TAPS, outs, lanes)
    stack = jnp.stack([lax.ppermute(w, ("dp", "tm"), pairs(k)) for k in range(h)], axis=1)
    stack = jnp.roll(stack, lax.axis_index("dp") % h, axis=1).reshape(TAPS, h * outs, lanes)
    rest = jnp.zeros((padded - TAPS * h * outs, lanes), BF16)
    joined = jnp.concatenate([stack[:, :main].reshape(-1, lanes), stack[:, main:].reshape(-1, lanes), rest])
    return lambda w: joined, after


def forward_kernel(two, w_ref, x_ref, s_ref, c_ref, *refs):
    if two:
        halos = [refs[:2]]
    else:
        halos = [refs[:2], refs[2:4]]
    bias_ref, thr_ref, gk_ref, gs_ref, rk_ref, rs_ref, p_ref = refs[2 * len(halos) :]
    core, row = lax.axis_index("tm"), lax.axis_index("rows")
    rows, times, cols, half = s_ref.shape
    lanes = x_ref.shape[2]
    steps = times // 2
    main, tail, _ = split_half(half)
    chunk = 16

    def half_row(ref):
        x = ref[...].reshape(1, 2 * half)
        return jnp.where(core == 0, x[:, :half], x[:, half:])

    thr = half_row(thr_ref)
    shift = half_row(bias_ref) - thr
    at_of = [lax.rem(core + part, 2) * steps + tl for part in range(2) for tl in range(steps)]

    def currents(x, strip):
        p = dot(x.reshape(-1, lanes), w_ref[...], ((1,), (1,)))
        p_ref[pl.ds(strip, 2)] = p.reshape(2, times * cols, -1)

    def scan(strip, cot, spike, g, h, keep=None):
        for w0 in range(0, cols, chunk):
            for lo, width, first in ((0, main, 0), (main, tail, TAPS * main)):
                th = thr[:, lo : lo + width]
                half_th = 0.5 * th
                sh = shift[:, lo : lo + width]
                state = jnp.zeros((chunk, width), F32)
                tanhs = []
                for t in range(times):
                    at = pl.ds(pl.multiple_of(at_of[t] * cols + w0, chunk), chunk)
                    now = sh
                    for dy in range(TAPS):
                        now = now + p_ref[strip + dy, at, first + dy * width : first + (dy + 1) * width]
                    y = state + now
                    tanh = jnp.tanh(y)
                    state = (y + half_th) - half_th * tanh
                    tanhs.append(tanh)
                adjoint = jnp.zeros((chunk, width), F32)
                grads, res = [None] * times, [None] * times
                for t in reversed(range(times)):
                    here = slice(w0, w0 + chunk), slice(lo, lo + width)
                    slope = 0.5 - 0.5 * (tanhs[t] * tanhs[t])
                    up = cot(at_of[t], here).astype(F32)
                    adjoint = adjoint + slope * (up - th * adjoint)
                    out = adjoint if keep is None else adjoint * keep
                    grads[t] = out.astype(BF16)
                    if h is not None:
                        fired = 0.5 + 0.5 * tanhs[t]
                        res[t] = (fired + spike(at_of[t], here).astype(F32)).astype(BF16)
                mine = core == 0
                for tl in range(steps):
                    a, b = grads[tl], grads[steps + tl]
                    gk_ref[tl, g, w0 : w0 + chunk, lo : lo + width] = jnp.where(mine, a, b)
                    gs_ref[tl, g, w0 : w0 + chunk, lo : lo + width] = jnp.where(mine, b, a)
                    if h is not None:
                        a, b = res[tl], res[steps + tl]
                        rk_ref[tl, h, w0 : w0 + chunk, lo : lo + width] = jnp.where(mine, a, b)
                        rs_ref[tl, h, w0 : w0 + chunk, lo : lo + width] = jnp.where(mine, b, a)

    def scan_own(h, strip):
        scan(
            strip,
            lambda at, here: c_ref[h, at, here[0], here[1]],
            lambda at, here: s_ref[h, at, here[0], here[1]],
            h + 1,
            h,
        )

    def scan_halo(n, strip, g, keep=None):
        scan(strip, lambda at, here: halos[n][1][at, here[0], here[1]], None, g, None, keep)

    if two:
        flip = row == 1
        edge_strip = jnp.where(flip, rows + 2, 0)
        edge = jnp.where(flip, rows + 1, 0)
        p_ref[edge_strip] = jnp.zeros(p_ref.shape[1:], F32)
        for ref in (gk_ref, gs_ref):
            for tl in range(steps):
                ref[tl, edge] = jnp.zeros((cols, half), BF16)

        def scan_at(j):
            if j == rows:
                scan_halo(0, jnp.where(flip, 0, rows), jnp.where(flip, 0, rows + 1))
            elif 0 <= j < rows:
                h = jnp.where(flip, rows - 1 - j, j)
                scan_own(h, jnp.where(flip, h + 1, h))

        done = 0
        for i in range(rows // 2 + 1):
            if i < rows // 2:
                h = jnp.where(flip, rows - 2 - 2 * i, 2 * i)
                currents(x_ref[pl.ds(h, 2)], jnp.where(flip, h + 2, h + 1))
            else:
                currents(halos[0][0][...], jnp.where(flip, 0, rows + 1))
            while done <= 2 * i - 2:
                scan_at(done)
                done += 1
        while done <= rows:
            scan_at(done)
            done += 1
    else:
        last = lax.axis_size("rows") - 1
        currents(halos[0][0][...], 0)
        currents(halos[1][0][...], rows + 2)

        def pair(i, carry):
            currents(x_ref[pl.ds(2 * i, 2)], 2 * i + 2)
            return carry

        lax.fori_loop(0, rows // 2, pair, 0)

        def one(h, carry):
            scan_own(h, h + 1)
            return carry

        lax.fori_loop(0, rows, one, 0)
        scan_halo(0, 0, 0, jnp.where(row == 0, 0.0, 1.0))
        scan_halo(1, rows + 1, rows + 1, jnp.where(row == last, 0.0, 1.0))


def forward(two, weights, taps, halo_taps, bias, thr):
    x, s, c = taps
    rows, times, cols, half = s.shape
    steps = times // 2
    args = [weights, x, s, c] + [a for pair in halo_taps for a in pair] + [bias, thr]
    grad = shape((steps, rows + 2, cols, half))
    res = shape((steps, rows, cols, half))
    return call(
        functools.partial(forward_kernel, two),
        (grad, grad, res, res),
        [VMEM_SPEC] * len(args),
        16,
        "forward",
        [pltpu.VMEM((rows + (3 if two else 4), times * cols, weights.shape[0]), F32)],
        cost=24 << 20,
    )(*args)


def rows_of_grads(g_ref, t, h0, count):
    cols, half = g_ref.shape[2:]
    main, tail, padded = split_half(half)
    taps = [g_ref[t, pl.ds(h0 + 2 - dy, count)].reshape(count * cols, half) for dy in range(TAPS)]
    rest = jnp.zeros((count * cols, padded - TAPS * half), BF16)
    return jnp.concatenate([x[:, :main] for x in taps] + [x[:, main:] for x in taps] + [rest], axis=1)


def backward_own_kernel(w_ref, g_ref, y_ref):
    steps, rows2 = g_ref.shape[:2]
    rows = rows2 - 2
    for t in range(steps):
        grads = rows_of_grads(g_ref, t, 0, rows)
        y_ref[t] = dot(grads, w_ref[...], ((1,), (0,)))


def backward_own(weights, grads):
    steps, rows2, cols, _ = grads.shape
    out = shape((steps, (rows2 - 2) * cols, weights.shape[1]), F32)
    return call(backward_own_kernel, out, [VMEM_SPEC] * 2, 12, "backward_own", cost=6 << 20)(weights, grads)


def backward_kernel(w_ref, g_ref, y_ref, cot_ref, rk_ref, rs_ref, out_ref, res_ref):
    t = pl.program_id(0)
    _, rows, cols, ch = cot_ref.shape
    core = lax.axis_index("tm")
    edge = lax.broadcasted_iota(jnp.int32, (1, cols, 1), 1)
    block = 4
    for h0 in range(0, rows, block):
        total = dot(rows_of_grads(g_ref, t, h0, block), w_ref[...], ((1,), (0,)))
        total = (total + y_ref[t, h0 * cols : (h0 + block) * cols, :]).reshape(block, cols, -1)
        left, mid, right = (total[:, :, k * ch : (k + 1) * ch] for k in range(TAPS))
        left = jnp.where(edge == cols - 1, 0.0, pltpu.roll(left, cols - 1, 1))
        right = jnp.where(edge == 0, 0.0, pltpu.roll(right, 1, 1))
        out_ref[0, h0 : h0 + block] = cot_ref[t, h0 : h0 + block].astype(F32) + (left + mid + right)
        a = rk_ref[t, h0 : h0 + block].astype(F32)
        b = rs_ref[t, h0 : h0 + block].astype(F32)
        both = jnp.concatenate([jnp.where(core == 0, a, b), jnp.where(core == 0, b, a)], axis=2)
        res_ref[0, h0 : h0 + block] = both.astype(BF16)


def backward(weights, grads, y, cot, res_keep, res_arrived):
    block = pl.BlockSpec((1,) + cot.shape[1:], lambda t: (t, 0, 0, 0))
    return call(
        backward_kernel,
        (shape(cot.shape, F32), shape(cot.shape)),
        [VMEM_SPEC] * 6,
        16,
        "backward",
        grid=(cot.shape[0],),
        out_specs=(block, block),
    )(weights, grads, y, cot, res_keep, res_arrived)


def swap_cores(x):
    return lax.ppermute(x, "tm", [(0, 1), (1, 0)])


def fetch_halos(two, halos):
    if two:
        return [lax.ppermute(halos[0], "rows", [(0, 1), (1, 0)])]
    count = lax.axis_size("rows")
    head, tail = halos
    return [
        lax.ppermute(tail, "rows", [(i, i + 1) for i in range(count - 1)]),
        lax.ppermute(head, "rows", [(i + 1, i) for i in range(count - 1)]),
    ]


def on_device(spikes, cotangent, weight_codes, block_exponents, current_bias, threshold):
    two = lax.axis_size("rows") == 2
    spikes, cot = spikes[0], cotangent[0]
    w, wq, wd, *halos = prepare(two, weight_codes, block_exponents, spikes, cot)
    lanes = QUARTERS * w.shape[2]
    halos = fetch_halos(two, halos)
    taps = build_taps(spikes, cot, swap_cores(spikes), swap_cores(cot), lanes)
    join, (taps, halos) = fetch_weights(w, wq, wd, (taps, halos))
    halo_taps = [build_halo_taps(x, swap_cores(x), lanes) for x in halos]
    w, taps, halo_taps = lax.optimization_barrier((w, taps, halo_taps))
    weights = join(w)
    weights2 = swap_cores(weights)
    keep, send, res_keep, res_send = forward(two, weights, taps, halo_taps, current_bias, threshold)
    arrived = swap_cores(send)
    res_arrived = swap_cores(res_send)
    y = backward_own(weights, keep)
    input_grad, residual = backward(weights2, arrived, y, cot, res_keep, res_arrived)
    return residual[None], input_grad[None]


def solution(mesh):
    return jax.shard_map(
        on_device,
        mesh=mesh,
        in_specs=(
            P(("groups", "dp"), "tm", "rows", None, None),
            P(("groups", "dp"), "tm", "rows", None, None),
            P(None, None, None, "dp"),
            P(None, None, None, "dp"),
            P(),
            P(),
        ),
        out_specs=(
            P(("groups", "dp"), "tm", "rows", None, None),
            P(("groups", "dp"), "tm", "rows", None, None),
        ),
        check_vma=False,
    )
```

```python
import functools

import jax
import jax.numpy as jnp
from jax import lax
from jax.experimental import pallas as pl
from jax.experimental.pallas import tpu as pltpu
from jax.sharding import PartitionSpec as P

MX_BLOCK = 32
TAPS = 3
F32 = jnp.float32
BF16 = jnp.bfloat16
VMEM_SPEC = pl.BlockSpec(memory_space=pltpu.VMEM)
HBM_SPEC = pl.BlockSpec(memory_space=pltpu.HBM)
QUARTERS = 4


def call(body, out_shape, in_specs, mib, name, scratch=(), grid=(), out_specs=None, cost=0):
    return pl.pallas_call(
        body,
        out_shape=out_shape,
        grid=grid,
        in_specs=in_specs,
        out_specs=out_specs or jax.tree.map(lambda _: VMEM_SPEC, out_shape),
        scratch_shapes=list(scratch),
        compiler_params=pltpu.CompilerParams(vmem_limit_bytes=mib << 20),
        cost_estimate=pl.CostEstimate(flops=0, transcendentals=0, bytes_accessed=cost) if cost else None,
        name=name,
    )


def in_hbm(x):
    return pltpu.with_memory_space_constraint(x, pltpu.HBM)


def shape(dims, dtype=BF16):
    return jax.ShapeDtypeStruct(dims, dtype)


def dot(a, b, dims):
    return lax.dot_general(a, b, (dims, ((), ())), preferred_element_type=F32)


def quarter_here():
    return lax.axis_index("groups") * 2 + lax.rem(lax.axis_index("rows"), 2)


def prepare_kernel(two, codes_hbm, exps_hbm, spikes_ref, cot_ref, *refs):
    w_ref, send_ref = refs[:2]
    halo_refs, (codes_ref, exps_ref, sems, code_sems) = refs[2:-4], refs[-4:]
    if two:
        halos = [(halo_refs[0], 1 - lax.axis_index("rows"))]
    else:
        halos = [(halo_refs[0], 0), (halo_refs[1], 1)]
    steps, rows = spikes_ref.shape[:2]
    scales = pltpu.make_async_copy(exps_hbm, exps_ref, code_sems.at[TAPS])
    codes = [pltpu.make_async_copy(codes_hbm.at[dy], codes_ref.at[dy], code_sems.at[dy]) for dy in range(TAPS)]
    scales.start()
    for copy in codes:
        copy.start()
    copies = []
    for n, (ref, end) in enumerate(halos):
        for t in range(steps):
            s = spikes_ref.at[t, pl.ds(end * (rows - 2), 2)]
            c = cot_ref.at[t, pl.ds(end * (rows - 1), 1)]
            copies.append(pltpu.make_async_copy(s, ref.at[t, pl.ds(0, 2)], sems.at[len(copies)]))
            copies.append(pltpu.make_async_copy(c, ref.at[t, pl.ds(2, 1)], sems.at[len(copies)]))
    for copy in copies:
        copy.start()
    outs, ins = codes_ref.shape[2:]
    blocks = exps_ref.shape[1]
    width = w_ref.shape[2]
    spread = lax.broadcasted_iota(jnp.int32, (blocks, ins), 1) // MX_BLOCK
    spread = (spread == lax.broadcasted_iota(jnp.int32, (blocks, ins), 0)).astype(F32).astype(BF16)
    scales.wait()
    for dy in range(TAPS):
        codes[dy].wait()
        parts = []
        for dx in range(TAPS):
            scale = 1.0 / lax.shift_left(jnp.int32(1), -exps_ref[dy, :, dx, :]).astype(F32)
            scale = dot(scale.astype(BF16), spread, ((0,), (0,)))
            parts.append(codes_ref[dy, dx].astype(F32) * scale)
        parts.append(jnp.zeros((outs, QUARTERS * width - TAPS * ins), F32))
        tap = jnp.concatenate(parts, axis=1).astype(BF16)
        for q in range(QUARTERS):
            w_ref[q, dy * outs : (dy + 1) * outs, :] = tap[:, q * width : (q + 1) * width]
    q = quarter_here()
    send_ref[: TAPS * outs] = w_ref[q]
    send_ref[TAPS * outs :] = w_ref[QUARTERS - 1 - q]
    for copy in copies:
        copy.wait()


def prepare(two, weight_codes, block_exponents, spikes, cot):
    outs = weight_codes.shape[3]
    steps, rows, cols, ch = spikes.shape
    width = -(-TAPS * ch // (QUARTERS * 128)) * 128
    n_halo = 1 if two else 2
    out = (shape((QUARTERS, TAPS * outs, width)), shape((2 * TAPS * outs, width))) + (shape((steps, 3, cols, ch)),) * n_halo
    return call(
        functools.partial(prepare_kernel, two),
        out,
        [HBM_SPEC] * 4,
        16,
        "prepare",
        [
            pltpu.VMEM((TAPS, TAPS, outs, ch), jnp.int32),
            pltpu.VMEM((TAPS, block_exponents.shape[2], TAPS, outs), jnp.int32),
            pltpu.SemaphoreType.DMA((2 * steps * n_halo,)),
            pltpu.SemaphoreType.DMA((TAPS + 1,)),
        ],
        cost=2 << 20,
    )(*map(in_hbm, (weight_codes.transpose(0, 1, 3, 2), block_exponents.transpose(0, 2, 1, 3), spikes, cot)))


def put_taps(x_ref, x, s, t):
    cols, ch = x.shape
    edge = lax.broadcasted_iota(jnp.int32, (cols, 1), 0)
    before = jnp.where(edge == 0, 0.0, pltpu.roll(x, 1, 0))
    after = jnp.where(edge == cols - 1, 0.0, pltpu.roll(x, cols - 1, 0))
    pad = jnp.zeros((cols, x_ref.shape[2] - TAPS * ch), F32)
    taps = jnp.concatenate([before, x, after, pad], axis=1)
    x_ref[s, pl.ds(pl.multiple_of(t * cols, cols), cols), :] = taps.astype(BF16)


def half_of(x):
    half = x.shape[-1] // 2
    return jnp.where(lax.axis_index("tm") == 0, x[:, :half], x[:, half:])


def taps_kernel(spikes_ref, spikes2_ref, cot_ref, cot2_ref, x_ref, s_ref, c_ref):
    steps, rows = spikes_ref.shape[:2]
    for which, (s_in, c_in) in enumerate(((spikes_ref, cot_ref), (spikes2_ref, cot2_ref))):

        def body(n, carry, s_in=s_in, c_in=c_in, which=which):
            t, h = n // rows, n % rows
            x = s_in[t, h].astype(F32)
            put_taps(x_ref, x, h, which * steps + t)
            s_ref[h, which * steps + t] = half_of(x).astype(BF16)
            c_ref[h, which * steps + t] = half_of(c_in[t, h].astype(F32)).astype(BF16)
            return carry

        lax.fori_loop(0, steps * rows, body, 0)


def build_taps(spikes, cot, spikes2, cot2, lanes):
    steps, rows, cols, ch = spikes.shape
    half = shape((rows, 2 * steps, cols, ch // 2))
    out = (shape((rows, 2 * steps * cols, lanes)), half, half)
    return call(taps_kernel, out, [VMEM_SPEC] * 4, 16, "taps", cost=18 << 20)(spikes, spikes2, cot, cot2)


def halo_taps_kernel(halo_ref, halo2_ref, x_ref, c_ref):
    steps = halo_ref.shape[0]
    for which, ref in enumerate((halo_ref, halo2_ref)):

        def body(t, carry, ref=ref, which=which):
            for k in range(2):
                put_taps(x_ref, ref[t, k].astype(F32), k, which * steps + t)
            c_ref[which * steps + t] = half_of(ref[t, 2].astype(F32)).astype(BF16)
            return carry

        lax.fori_loop(0, steps, body, 0)


def build_halo_taps(halo, halo2, lanes):
    steps, _, cols, ch = halo.shape
    out = (shape((2, 2 * steps * cols, lanes)), shape((2 * steps, cols, ch // 2)))
    return call(halo_taps_kernel, out, [VMEM_SPEC] * 2, 16, "halo_taps", cost=2 << 20)(halo, halo2)


def split_half(half):
    main = half // 128 * 128
    return main, half - main, TAPS * main + -(-TAPS * (half - main) // 128) * 128


def join_kernel(w_ref, *refs):
    rounds, x_ref, y_ref, out_ref = refs[:2], refs[2], refs[3], refs[4]
    size = w_ref.shape[1]
    halves = [pl.ds(k * size, size) for k in range(2)]
    rounds = [(rounds[k].at[halves[0]], rounds[k].at[halves[1]], x_ref.at[halves[k]], y_ref.at[halves[k]]) for k in range(2)]
    outs = w_ref.shape[1] // TAPS
    width = w_ref.shape[2]
    main, tail, _ = split_half(2 * outs)
    z, core, q = lax.axis_index("dp"), lax.axis_index("tm"), quarter_here()
    place = lax.rem(z, 2)
    own = core == z // 2

    def put(part, lane, pos):
        at = pl.ds(pl.multiple_of(lane * width, width), width)
        for dy in range(TAPS):
            for o in range(0, outs, 16):
                c = pos * outs + o
                to = dy * main + c if c < main else TAPS * main + dy * tail + c - main
                out_ref[to : to + 16, at] = part[dy * outs + o : dy * outs + o + 16, :]

    def put_round(k, pos):
        lanes_of = (q, QUARTERS - 1 - q, jnp.bitwise_xor(q, 1), jnp.bitwise_xor(q, 2))
        if k == 1:
            for part, lane in zip(rounds[1], lanes_of):
                put(part, lane, pos)
            return

        @pl.when(own)
        def _():
            for n in range(QUARTERS):
                put(w_ref[n], n, pos)

        @pl.when(jnp.logical_not(own))
        def _():
            for part, lane in zip(rounds[0], lanes_of):
                put(part, lane, pos)

    for even in range(2):

        @pl.when(place == even)
        def _():
            put_round(0, even)
            put_round(1, 1 - even)

    rest = out_ref.shape[0] - TAPS * 2 * outs
    out_ref[TAPS * 2 * outs :, :] = jnp.zeros((rest, out_ref.shape[1]), BF16)


def fetch_weights(w, send, after):
    count = lax.axis_size("dp")
    n_rows = lax.axis_size("rows")
    h = count // 2
    outs = w.shape[1] // TAPS
    lanes = QUARTERS * w.shape[2]

    def pairs(k):
        todo = []
        for z in range(count):
            for c in range(2):
                s = c * h + (z + k) % h
                todo.append((s * 2 + z // h, z * 2 + c))
        return todo

    main, tail, padded = split_half(h * outs)
    if h == 2 and outs % 16 == 0 and n_rows % 2 == 0 and lax.axis_size("groups") == 2:
        moved = [[(a, b) for a, b in pairs(k) if a != b] for k in range(h)]
        rounds = [lax.ppermute(send, ("dp", "tm"), moved[k]) for k in range(h)]
        rounds, after = lax.optimization_barrier((rounds, after))
        both = jnp.concatenate([r[: TAPS * outs] for r in rounds])
        x = lax.ppermute(both, "rows", [(r, r ^ 1) for r in range(n_rows)])
        y = lax.ppermute(both, "groups", [(0, 1), (1, 0)])
        return lambda w: call(join_kernel, shape((padded, lanes)), [VMEM_SPEC] * 5, 8, "join")(w, *rounds, x, y), after
    w = w.reshape(QUARTERS, TAPS, outs, -1).transpose(1, 2, 0, 3).reshape(TAPS, outs, lanes)
    stack = jnp.stack([lax.ppermute(w, ("dp", "tm"), pairs(k)) for k in range(h)], axis=1)
    stack = jnp.roll(stack, lax.axis_index("dp") % h, axis=1).reshape(TAPS, h * outs, lanes)
    rest = jnp.zeros((padded - TAPS * h * outs, lanes), BF16)
    joined = jnp.concatenate([stack[:, :main].reshape(-1, lanes), stack[:, main:].reshape(-1, lanes), rest])
    return lambda w: joined, after


def forward_kernel(two, w_ref, x_ref, s_ref, c_ref, *refs):
    if two:
        halos = [refs[:2]]
    else:
        halos = [refs[:2], refs[2:4]]
    bias_ref, thr_ref, gk_ref, gs_ref, rk_ref, rs_ref, p_ref = refs[2 * len(halos) :]
    core, row = lax.axis_index("tm"), lax.axis_index("rows")
    rows, times, cols, half = s_ref.shape
    lanes = x_ref.shape[2]
    steps = times // 2
    main, tail, _ = split_half(half)
    chunk = 16

    def half_row(ref):
        x = ref[...].reshape(1, 2 * half)
        return jnp.where(core == 0, x[:, :half], x[:, half:])

    thr = half_row(thr_ref)
    shift = half_row(bias_ref) - thr
    at_of = [lax.rem(core + part, 2) * steps + tl for part in range(2) for tl in range(steps)]

    def currents(x, strip):
        p = dot(x.reshape(-1, lanes), w_ref[...], ((1,), (1,)))
        p_ref[pl.ds(strip, 2)] = p.reshape(2, times * cols, -1)

    def scan(strip, cot, spike, g, h, keep=None):
        for w0 in range(0, cols, chunk):
            for lo, width, first in ((0, main, 0), (main, tail, TAPS * main)):
                th = thr[:, lo : lo + width]
                half_th = 0.5 * th
                sh = shift[:, lo : lo + width]
                state = jnp.zeros((chunk, width), F32)
                tanhs = []
                for t in range(times):
                    at = pl.ds(pl.multiple_of(at_of[t] * cols + w0, chunk), chunk)
                    now = sh
                    for dy in range(TAPS):
                        now = now + p_ref[strip + dy, at, first + dy * width : first + (dy + 1) * width]
                    y = state + now
                    tanh = jnp.tanh(y)
                    state = (y + half_th) - half_th * tanh
                    tanhs.append(tanh)
                adjoint = jnp.zeros((chunk, width), F32)
                grads, res = [None] * times, [None] * times
                for t in reversed(range(times)):
                    here = slice(w0, w0 + chunk), slice(lo, lo + width)
                    slope = 0.5 - 0.5 * (tanhs[t] * tanhs[t])
                    up = cot(at_of[t], here).astype(F32)
                    adjoint = adjoint + slope * (up - th * adjoint)
                    out = adjoint if keep is None else adjoint * keep
                    grads[t] = out.astype(BF16)
                    if h is not None:
                        fired = 0.5 + 0.5 * tanhs[t]
                        res[t] = (fired + spike(at_of[t], here).astype(F32)).astype(BF16)
                mine = core == 0
                for tl in range(steps):
                    a, b = grads[tl], grads[steps + tl]
                    gk_ref[tl, g, w0 : w0 + chunk, lo : lo + width] = jnp.where(mine, a, b)
                    gs_ref[tl, g, w0 : w0 + chunk, lo : lo + width] = jnp.where(mine, b, a)
                    if h is not None:
                        a, b = res[tl], res[steps + tl]
                        rk_ref[tl, h, w0 : w0 + chunk, lo : lo + width] = jnp.where(mine, a, b)
                        rs_ref[tl, h, w0 : w0 + chunk, lo : lo + width] = jnp.where(mine, b, a)

    def scan_own(h, strip):
        scan(
            strip,
            lambda at, here: c_ref[h, at, here[0], here[1]],
            lambda at, here: s_ref[h, at, here[0], here[1]],
            h + 1,
            h,
        )

    def scan_halo(n, strip, g, keep=None):
        scan(strip, lambda at, here: halos[n][1][at, here[0], here[1]], None, g, None, keep)

    if two:
        flip = row == 1
        edge_strip = jnp.where(flip, rows + 2, 0)
        edge = jnp.where(flip, rows + 1, 0)
        p_ref[edge_strip] = jnp.zeros(p_ref.shape[1:], F32)
        for ref in (gk_ref, gs_ref):
            for tl in range(steps):
                ref[tl, edge] = jnp.zeros((cols, half), BF16)

        def scan_at(j):
            if j == rows:
                scan_halo(0, jnp.where(flip, 0, rows), jnp.where(flip, 0, rows + 1))
            elif 0 <= j < rows:
                h = jnp.where(flip, rows - 1 - j, j)
                scan_own(h, jnp.where(flip, h + 1, h))

        done = 0
        for i in range(rows // 2 + 1):
            if i < rows // 2:
                h = jnp.where(flip, rows - 2 - 2 * i, 2 * i)
                currents(x_ref[pl.ds(h, 2)], jnp.where(flip, h + 2, h + 1))
            else:
                currents(halos[0][0][...], jnp.where(flip, 0, rows + 1))
            while done <= 2 * i - 2:
                scan_at(done)
                done += 1
        while done <= rows:
            scan_at(done)
            done += 1
    else:
        last = lax.axis_size("rows") - 1
        currents(halos[0][0][...], 0)
        currents(halos[1][0][...], rows + 2)

        def pair(i, carry):
            currents(x_ref[pl.ds(2 * i, 2)], 2 * i + 2)
            return carry

        lax.fori_loop(0, rows // 2, pair, 0)

        def one(h, carry):
            scan_own(h, h + 1)
            return carry

        lax.fori_loop(0, rows, one, 0)
        scan_halo(0, 0, 0, jnp.where(row == 0, 0.0, 1.0))
        scan_halo(1, rows + 1, rows + 1, jnp.where(row == last, 0.0, 1.0))


def forward(two, weights, taps, halo_taps, bias, thr):
    x, s, c = taps
    rows, times, cols, half = s.shape
    steps = times // 2
    args = [weights, x, s, c] + [a for pair in halo_taps for a in pair] + [bias, thr]
    grad = shape((steps, rows + 2, cols, half))
    res = shape((steps, rows, cols, half))
    return call(
        functools.partial(forward_kernel, two),
        (grad, grad, res, res),
        [VMEM_SPEC] * len(args),
        16,
        "forward",
        [pltpu.VMEM((rows + (3 if two else 4), times * cols, weights.shape[0]), F32)],
        cost=24 << 20,
    )(*args)


def rows_of_grads(g_ref, t, h0, count):
    cols, half = g_ref.shape[2:]
    main, tail, padded = split_half(half)
    taps = [g_ref[t, pl.ds(h0 + 2 - dy, count)].reshape(count * cols, half) for dy in range(TAPS)]
    rest = jnp.zeros((count * cols, padded - TAPS * half), BF16)
    return jnp.concatenate([x[:, :main] for x in taps] + [x[:, main:] for x in taps] + [rest], axis=1)


def backward_own_kernel(w_ref, g_ref, y_ref):
    steps, rows2 = g_ref.shape[:2]
    rows = rows2 - 2
    for t in range(steps):
        grads = rows_of_grads(g_ref, t, 0, rows)
        y_ref[t] = dot(grads, w_ref[...], ((1,), (0,)))


def backward_own(weights, grads):
    steps, rows2, cols, _ = grads.shape
    out = shape((steps, (rows2 - 2) * cols, weights.shape[1]), F32)
    return call(backward_own_kernel, out, [VMEM_SPEC] * 2, 12, "backward_own", cost=6 << 20)(weights, grads)


def backward_kernel(w_ref, g_ref, y_ref, cot_ref, rk_ref, rs_ref, out_ref, res_ref):
    t = pl.program_id(0)
    _, rows, cols, ch = cot_ref.shape
    core = lax.axis_index("tm")
    edge = lax.broadcasted_iota(jnp.int32, (1, cols, 1), 1)
    block = 4
    for h0 in range(0, rows, block):
        total = dot(rows_of_grads(g_ref, t, h0, block), w_ref[...], ((1,), (0,)))
        total = (total + y_ref[t, h0 * cols : (h0 + block) * cols, :]).reshape(block, cols, -1)
        left, mid, right = (total[:, :, k * ch : (k + 1) * ch] for k in range(TAPS))
        left = jnp.where(edge == cols - 1, 0.0, pltpu.roll(left, cols - 1, 1))
        right = jnp.where(edge == 0, 0.0, pltpu.roll(right, 1, 1))
        out_ref[0, h0 : h0 + block] = cot_ref[t, h0 : h0 + block].astype(F32) + (left + mid + right)
        a = rk_ref[t, h0 : h0 + block].astype(F32)
        b = rs_ref[t, h0 : h0 + block].astype(F32)
        both = jnp.concatenate([jnp.where(core == 0, a, b), jnp.where(core == 0, b, a)], axis=2)
        res_ref[0, h0 : h0 + block] = both.astype(BF16)


def backward(weights, grads, y, cot, res_keep, res_arrived):
    block = pl.BlockSpec((1,) + cot.shape[1:], lambda t: (t, 0, 0, 0))
    return call(
        backward_kernel,
        (shape(cot.shape, F32), shape(cot.shape)),
        [VMEM_SPEC] * 6,
        16,
        "backward",
        grid=(cot.shape[0],),
        out_specs=(block, block),
    )(weights, grads, y, cot, res_keep, res_arrived)


def swap_cores(x):
    return lax.ppermute(x, "tm", [(0, 1), (1, 0)])


def fetch_halos(two, halos):
    if two:
        return [lax.ppermute(halos[0], "rows", [(0, 1), (1, 0)])]
    count = lax.axis_size("rows")
    head, tail = halos
    return [
        lax.ppermute(tail, "rows", [(i, i + 1) for i in range(count - 1)]),
        lax.ppermute(head, "rows", [(i + 1, i) for i in range(count - 1)]),
    ]


def on_device(spikes, cotangent, weight_codes, block_exponents, current_bias, threshold):
    two = lax.axis_size("rows") == 2
    spikes, cot = spikes[0], cotangent[0]
    w, send, *halos = prepare(two, weight_codes, block_exponents, spikes, cot)
    lanes = QUARTERS * w.shape[2]
    halos = fetch_halos(two, halos)
    taps = build_taps(spikes, cot, swap_cores(spikes), swap_cores(cot), lanes)
    taps, halos = lax.optimization_barrier((taps, halos))
    join, taps = fetch_weights(w, send, taps)
    halo_taps = [build_halo_taps(x, swap_cores(x), lanes) for x in halos]
    w, taps, halo_taps = lax.optimization_barrier((w, taps, halo_taps))
    weights = join(w)
    weights2 = swap_cores(weights)
    keep, send, res_keep, res_send = forward(two, weights, taps, halo_taps, current_bias, threshold)
    arrived = swap_cores(send)
    res_arrived = swap_cores(res_send)
    y = backward_own(weights, keep)
    input_grad, residual = backward(weights2, arrived, y, cot, res_keep, res_arrived)
    return residual[None], input_grad[None]


def solution(mesh):
    return jax.shard_map(
        on_device,
        mesh=mesh,
        in_specs=(
            P(("groups", "dp"), "tm", "rows", None, None),
            P(("groups", "dp"), "tm", "rows", None, None),
            P(None, None, None, "dp"),
            P(None, None, None, "dp"),
            P(),
            P(),
        ),
        out_specs=(
            P(("groups", "dp"), "tm", "rows", None, None),
            P(("groups", "dp"), "tm", "rows", None, None),
        ),
        check_vma=False,
    )
```

```python
import functools

import jax
import jax.numpy as jnp
from jax import lax
from jax.experimental import pallas as pl
from jax.experimental.pallas import tpu as pltpu
from jax.sharding import PartitionSpec as P

MX_BLOCK = 32
TAPS = 3
F32 = jnp.float32
BF16 = jnp.bfloat16
VMEM_SPEC = pl.BlockSpec(memory_space=pltpu.VMEM)
HBM_SPEC = pl.BlockSpec(memory_space=pltpu.HBM)
QUARTERS = 4


def call(body, out_shape, in_specs, mib, name, scratch=(), grid=(), out_specs=None, cost=0):
    return pl.pallas_call(
        body,
        out_shape=out_shape,
        grid=grid,
        in_specs=in_specs,
        out_specs=out_specs or jax.tree.map(lambda _: VMEM_SPEC, out_shape),
        scratch_shapes=list(scratch),
        compiler_params=pltpu.CompilerParams(vmem_limit_bytes=mib << 20),
        cost_estimate=pl.CostEstimate(flops=0, transcendentals=0, bytes_accessed=cost) if cost else None,
        name=name,
    )


def in_hbm(x):
    return pltpu.with_memory_space_constraint(x, pltpu.HBM)


def shape(dims, dtype=BF16):
    return jax.ShapeDtypeStruct(dims, dtype)


def dot(a, b, dims):
    return lax.dot_general(a, b, (dims, ((), ())), preferred_element_type=F32)


def quarter_here():
    return lax.axis_index("groups") * 2 + lax.rem(lax.axis_index("rows"), 2)


def prepare_kernel(two, codes_hbm, exps_hbm, spikes_ref, cot_ref, *refs):
    w_ref, send_ref = refs[:2]
    halo_refs, (codes_ref, exps_ref, sems, code_sems) = refs[2:-4], refs[-4:]
    if two:
        halos = [(halo_refs[0], 1 - lax.axis_index("rows"))]
    else:
        halos = [(halo_refs[0], 0), (halo_refs[1], 1)]
    steps, rows = spikes_ref.shape[:2]
    scales = pltpu.make_async_copy(exps_hbm, exps_ref, code_sems.at[TAPS])
    codes = [pltpu.make_async_copy(codes_hbm.at[dy], codes_ref.at[dy], code_sems.at[dy]) for dy in range(TAPS)]
    scales.start()
    for copy in codes:
        copy.start()
    copies = []
    for n, (ref, end) in enumerate(halos):
        for t in range(steps):
            s = spikes_ref.at[t, pl.ds(end * (rows - 2), 2)]
            c = cot_ref.at[t, pl.ds(end * (rows - 1), 1)]
            copies.append(pltpu.make_async_copy(s, ref.at[t, pl.ds(0, 2)], sems.at[len(copies)]))
            copies.append(pltpu.make_async_copy(c, ref.at[t, pl.ds(2, 1)], sems.at[len(copies)]))
    for copy in copies:
        copy.start()
    outs, ins = codes_ref.shape[2:]
    blocks = exps_ref.shape[1]
    width = w_ref.shape[2]
    spread = lax.broadcasted_iota(jnp.int32, (blocks, ins), 1) // MX_BLOCK
    spread = (spread == lax.broadcasted_iota(jnp.int32, (blocks, ins), 0)).astype(F32).astype(BF16)
    scales.wait()
    for dy in range(TAPS):
        codes[dy].wait()
        parts = []
        for dx in range(TAPS):
            scale = 1.0 / lax.shift_left(jnp.int32(1), -exps_ref[dy, :, dx, :]).astype(F32)
            scale = dot(scale.astype(BF16), spread, ((0,), (0,)))
            parts.append(codes_ref[dy, dx].astype(F32) * scale)
        parts.append(jnp.zeros((outs, QUARTERS * width - TAPS * ins), F32))
        tap = jnp.concatenate(parts, axis=1).astype(BF16)
        for q in range(QUARTERS):
            w_ref[q, dy * outs : (dy + 1) * outs, :] = tap[:, q * width : (q + 1) * width]
    q = quarter_here()
    send_ref[: TAPS * outs] = w_ref[q]
    send_ref[TAPS * outs :] = w_ref[QUARTERS - 1 - q]
    for copy in copies:
        copy.wait()


def prepare(two, weight_codes, block_exponents, spikes, cot):
    outs = weight_codes.shape[3]
    steps, rows, cols, ch = spikes.shape
    width = -(-TAPS * ch // (QUARTERS * 128)) * 128
    n_halo = 1 if two else 2
    out = (shape((QUARTERS, TAPS * outs, width)), shape((2 * TAPS * outs, width))) + (shape((steps, 3, cols, ch)),) * n_halo
    return call(
        functools.partial(prepare_kernel, two),
        out,
        [HBM_SPEC] * 4,
        16,
        "prepare",
        [
            pltpu.VMEM((TAPS, TAPS, outs, ch), jnp.int32),
            pltpu.VMEM((TAPS, block_exponents.shape[2], TAPS, outs), jnp.int32),
            pltpu.SemaphoreType.DMA((2 * steps * n_halo,)),
            pltpu.SemaphoreType.DMA((TAPS + 1,)),
        ],
        cost=2 << 20,
    )(*map(in_hbm, (weight_codes.transpose(0, 1, 3, 2), block_exponents.transpose(0, 2, 1, 3), spikes, cot)))


def put_taps(x_ref, x, s, t):
    cols, ch = x.shape
    edge = lax.broadcasted_iota(jnp.int32, (cols, 1), 0)
    before = jnp.where(edge == 0, 0.0, pltpu.roll(x, 1, 0))
    after = jnp.where(edge == cols - 1, 0.0, pltpu.roll(x, cols - 1, 0))
    pad = jnp.zeros((cols, x_ref.shape[2] - TAPS * ch), F32)
    taps = jnp.concatenate([before, x, after, pad], axis=1)
    x_ref[s, pl.ds(pl.multiple_of(t * cols, cols), cols), :] = taps.astype(BF16)


def half_of(x):
    half = x.shape[-1] // 2
    return jnp.where(lax.axis_index("tm") == 0, x[:, :half], x[:, half:])


def taps_kernel(spikes_ref, spikes2_ref, cot_ref, cot2_ref, x_ref, s_ref, c_ref):
    steps, rows = spikes_ref.shape[:2]
    for which, (s_in, c_in) in enumerate(((spikes_ref, cot_ref), (spikes2_ref, cot2_ref))):

        def body(n, carry, s_in=s_in, c_in=c_in, which=which):
            t, h = n // rows, n % rows
            x = s_in[t, h].astype(F32)
            put_taps(x_ref, x, h, which * steps + t)
            s_ref[h, which * steps + t] = half_of(x).astype(BF16)
            c_ref[h, which * steps + t] = half_of(c_in[t, h].astype(F32)).astype(BF16)
            return carry

        lax.fori_loop(0, steps * rows, body, 0)


def build_taps(spikes, cot, spikes2, cot2, lanes):
    steps, rows, cols, ch = spikes.shape
    half = shape((rows, 2 * steps, cols, ch // 2))
    out = (shape((rows, 2 * steps * cols, lanes)), half, half)
    return call(taps_kernel, out, [VMEM_SPEC] * 4, 16, "taps", cost=18 << 20)(spikes, spikes2, cot, cot2)


def halo_taps_kernel(halo_ref, halo2_ref, x_ref, c_ref):
    steps = halo_ref.shape[0]
    for which, ref in enumerate((halo_ref, halo2_ref)):

        def body(t, carry, ref=ref, which=which):
            for k in range(2):
                put_taps(x_ref, ref[t, k].astype(F32), k, which * steps + t)
            c_ref[which * steps + t] = half_of(ref[t, 2].astype(F32)).astype(BF16)
            return carry

        lax.fori_loop(0, steps, body, 0)


def build_halo_taps(halo, halo2, lanes):
    steps, _, cols, ch = halo.shape
    out = (shape((2, 2 * steps * cols, lanes)), shape((2 * steps, cols, ch // 2)))
    return call(halo_taps_kernel, out, [VMEM_SPEC] * 2, 16, "halo_taps", cost=2 << 20)(halo, halo2)


def split_half(half):
    main = half // 128 * 128
    return main, half - main, TAPS * main + -(-TAPS * (half - main) // 128) * 128


def put_rows(out_ref, part, lane, pos):
    outs, width = part.shape[0] // TAPS, part.shape[1]
    main, tail, _ = split_half(2 * outs)
    at = pl.ds(pl.multiple_of(lane * width, width), width)
    for dy in range(TAPS):
        for o in range(0, outs, 16):
            c = pos * outs + o
            to = dy * main + c if c < main else TAPS * main + dy * tail + c - main
            out_ref[to : to + 16, at] = part[dy * outs + o : dy * outs + o + 16, :]


def put_shards(out_ref, own_parts, rounds):
    z, core = lax.axis_index("dp"), lax.axis_index("tm")
    own = core == z // 2

    def put_all(parts, pos):
        for part, lane in parts:
            put_rows(out_ref, part, lane, pos)

    for even in range(2):

        @pl.when(lax.rem(z, 2) == even)
        def _():
            pl.when(own)(lambda: put_all(own_parts, even))
            pl.when(jnp.logical_not(own))(lambda: put_all(rounds[0], even))
            put_all(rounds[1], 1 - even)

    used = 2 * rounds[0][0][0].shape[0]
    out_ref[used:, :] = jnp.zeros((out_ref.shape[0] - used, out_ref.shape[1]), BF16)


def lanes_here():
    q = quarter_here()
    return (q, QUARTERS - 1 - q), (jnp.bitwise_xor(q, 1), jnp.bitwise_xor(q, 2))


def join_kernel(w_ref, first_ref, second_ref, x_ref, y_ref, out_ref):
    size = w_ref.shape[1]
    halves = [pl.ds(k * size, size) for k in range(2)]
    here, there = lanes_here()
    rounds = []
    for k, ref in enumerate((first_ref, second_ref)):
        parts = ref.at[halves[0]], ref.at[halves[1]], x_ref.at[halves[k]], y_ref.at[halves[k]]
        rounds.append(list(zip(parts, here + there)))
    put_shards(out_ref, [(w_ref.at[n], n) for n in range(QUARTERS)], rounds)


def partial_kernel(w_ref, first_ref, second_ref, x_ref, halo_ref, p_ref, wh_ref):
    size, width = w_ref.shape[1:]
    halves = [pl.ds(k * size, size) for k in range(2)]
    here, _ = lanes_here()
    rounds = [[(ref.at[halves[n]], n) for n in range(2)] for ref in (first_ref, second_ref)]
    put_shards(wh_ref, [(w_ref.at[here[n]], n) for n in range(2)], rounds)
    for x, h, strip in strips(x_ref, halo_ref):
        p_ref[pl.ds(strip, 2)] = dot(take_lanes(x, h, here, width), wh_ref[...], ((1,), (1,))).reshape(2, -1, wh_ref.shape[0])


def take_lanes(x, h, lanes, width):
    parts = [x[pl.ds(h, 2), :, pl.ds(pl.multiple_of(n * width, width), width)] for n in lanes]
    return jnp.concatenate([part.reshape(-1, width) for part in parts], axis=1)


def strips(x_ref, halo_ref):
    rows = x_ref.shape[0]
    flip = lax.axis_index("rows") == 1
    todo = []
    for i in range(0, rows, 2):
        h = jnp.where(flip, rows - 2 - i, i)
        todo.append((x_ref, h, jnp.where(flip, h + 2, h + 1)))
    return todo + [(halo_ref, 0, jnp.where(flip, 0, rows + 1))]


def partial_currents(two, w, rounds, taps, halo_taps):
    x = taps[0]
    main, tail, padded = split_half(2 * w.shape[1] // TAPS)
    out = shape((x.shape[0] + 3, x.shape[1], padded), F32)
    scratch = [pltpu.VMEM((padded, 2 * w.shape[2]), BF16)]
    return call(partial_kernel, out, [VMEM_SPEC] * 5, 12, "partial", scratch)(w, *rounds, x, halo_taps[0][0])


def fetch_weights(w, send, after):
    count = lax.axis_size("dp")
    n_rows = lax.axis_size("rows")
    h = count // 2
    outs = w.shape[1] // TAPS
    lanes = QUARTERS * w.shape[2]

    def pairs(k):
        todo = []
        for z in range(count):
            for c in range(2):
                s = c * h + (z + k) % h
                todo.append((s * 2 + z // h, z * 2 + c))
        return todo

    main, tail, padded = split_half(h * outs)
    if h == 2 and outs % 16 == 0 and n_rows % 2 == 0 and lax.axis_size("groups") == 2:
        moved = [[(a, b) for a, b in pairs(k) if a != b] for k in range(h)]
        rounds = [lax.ppermute(send, ("dp", "tm"), moved[k]) for k in range(h)]
        rounds, after = lax.optimization_barrier((rounds, after))
        first = functools.partial(partial_currents, True, w, rounds) if n_rows == 2 else None
        both = jnp.concatenate([r[: TAPS * outs] for r in rounds])
        x = lax.ppermute(both, "rows", [(r, r ^ 1) for r in range(n_rows)])
        y = lax.ppermute(both, "groups", [(0, 1), (1, 0)])
        return lambda w: call(join_kernel, shape((padded, lanes)), [VMEM_SPEC] * 5, 8, "join")(w, *rounds, x, y), after, first
    w = w.reshape(QUARTERS, TAPS, outs, -1).transpose(1, 2, 0, 3).reshape(TAPS, outs, lanes)
    stack = jnp.stack([lax.ppermute(w, ("dp", "tm"), pairs(k)) for k in range(h)], axis=1)
    stack = jnp.roll(stack, lax.axis_index("dp") % h, axis=1).reshape(TAPS, h * outs, lanes)
    rest = jnp.zeros((padded - TAPS * h * outs, lanes), BF16)
    joined = jnp.concatenate([stack[:, :main].reshape(-1, lanes), stack[:, main:].reshape(-1, lanes), rest])
    return lambda w: joined, after, None


def forward_kernel(two, started, w_ref, x_ref, s_ref, c_ref, *refs):
    if two:
        halos = [refs[:2]]
    else:
        halos = [refs[:2], refs[2:4]]
    bias_ref, thr_ref, *begun, gk_ref, gs_ref, rk_ref, rs_ref, p_ref = refs[2 * len(halos) :]
    core, row = lax.axis_index("tm"), lax.axis_index("rows")
    rows, times, cols, half = s_ref.shape
    lanes = x_ref.shape[2]
    steps = times // 2
    main, tail, _ = split_half(half)
    chunk = 16

    def half_row(ref):
        x = ref[...].reshape(1, 2 * half)
        return jnp.where(core == 0, x[:, :half], x[:, half:])

    thr = half_row(thr_ref)
    shift = half_row(bias_ref) - thr
    at_of = [lax.rem(core + part, 2) * steps + tl for part in range(2) for tl in range(steps)]

    if started:
        _, there = lanes_here()
        width = lanes // QUARTERS
        w_there = jnp.concatenate([w_ref[:, pl.ds(pl.multiple_of(n * width, width), width)] for n in there], axis=1)

    def currents(x, h, strip):
        if started:
            p = dot(take_lanes(x, h, there, width), w_there, ((1,), (1,)))
            p_ref[pl.ds(strip, 2)] = begun[0][pl.ds(strip, 2)] + p.reshape(2, times * cols, -1)
        else:
            p = dot(x[pl.ds(h, 2)].reshape(-1, lanes), w_ref[...], ((1,), (1,)))
            p_ref[pl.ds(strip, 2)] = p.reshape(2, times * cols, -1)

    def scan(strip, cot, spike, g, h, keep=None):
        for w0 in range(0, cols, chunk):
            for lo, width, first in ((0, main, 0), (main, tail, TAPS * main)):
                th = thr[:, lo : lo + width]
                half_th = 0.5 * th
                sh = shift[:, lo : lo + width]
                state = jnp.zeros((chunk, width), F32)
                tanhs = []
                for t in range(times):
                    at = pl.ds(pl.multiple_of(at_of[t] * cols + w0, chunk), chunk)
                    now = sh
                    for dy in range(TAPS):
                        now = now + p_ref[strip + dy, at, first + dy * width : first + (dy + 1) * width]
                    y = state + now
                    tanh = jnp.tanh(y)
                    state = (y + half_th) - half_th * tanh
                    tanhs.append(tanh)
                adjoint = jnp.zeros((chunk, width), F32)
                grads, res = [None] * times, [None] * times
                for t in reversed(range(times)):
                    here = slice(w0, w0 + chunk), slice(lo, lo + width)
                    slope = 0.5 - 0.5 * (tanhs[t] * tanhs[t])
                    up = cot(at_of[t], here).astype(F32)
                    adjoint = adjoint + slope * (up - th * adjoint)
                    out = adjoint if keep is None else adjoint * keep
                    grads[t] = out.astype(BF16)
                    if h is not None:
                        fired = 0.5 + 0.5 * tanhs[t]
                        res[t] = (fired + spike(at_of[t], here).astype(F32)).astype(BF16)
                mine = core == 0
                for tl in range(steps):
                    a, b = grads[tl], grads[steps + tl]
                    gk_ref[tl, g, w0 : w0 + chunk, lo : lo + width] = jnp.where(mine, a, b)
                    gs_ref[tl, g, w0 : w0 + chunk, lo : lo + width] = jnp.where(mine, b, a)
                    if h is not None:
                        a, b = res[tl], res[steps + tl]
                        rk_ref[tl, h, w0 : w0 + chunk, lo : lo + width] = jnp.where(mine, a, b)
                        rs_ref[tl, h, w0 : w0 + chunk, lo : lo + width] = jnp.where(mine, b, a)

    def scan_own(h, strip):
        scan(
            strip,
            lambda at, here: c_ref[h, at, here[0], here[1]],
            lambda at, here: s_ref[h, at, here[0], here[1]],
            h + 1,
            h,
        )

    def scan_halo(n, strip, g, keep=None):
        scan(strip, lambda at, here: halos[n][1][at, here[0], here[1]], None, g, None, keep)

    if two:
        flip = row == 1
        edge_strip = jnp.where(flip, rows + 2, 0)
        edge = jnp.where(flip, rows + 1, 0)
        p_ref[edge_strip] = jnp.zeros(p_ref.shape[1:], F32)
        for ref in (gk_ref, gs_ref):
            for tl in range(steps):
                ref[tl, edge] = jnp.zeros((cols, half), BF16)

        def scan_at(j):
            if j == rows:
                scan_halo(0, jnp.where(flip, 0, rows), jnp.where(flip, 0, rows + 1))
            elif 0 <= j < rows:
                h = jnp.where(flip, rows - 1 - j, j)
                scan_own(h, jnp.where(flip, h + 1, h))

        done = 0
        for i, (x, h, strip) in enumerate(strips(x_ref, halos[0][0])):
            currents(x, h, strip)
            while done <= 2 * i - 2:
                scan_at(done)
                done += 1
        while done <= rows:
            scan_at(done)
            done += 1
    else:
        last = lax.axis_size("rows") - 1
        currents(halos[0][0], 0, 0)
        currents(halos[1][0], 0, rows + 2)

        def pair(i, carry):
            currents(x_ref, 2 * i, 2 * i + 2)
            return carry

        lax.fori_loop(0, rows // 2, pair, 0)

        def one(h, carry):
            scan_own(h, h + 1)
            return carry

        lax.fori_loop(0, rows, one, 0)
        scan_halo(0, 0, 0, jnp.where(row == 0, 0.0, 1.0))
        scan_halo(1, rows + 1, rows + 1, jnp.where(row == last, 0.0, 1.0))


def forward(two, weights, taps, halo_taps, bias, thr, begun=()):
    x, s, c = taps
    rows, times, cols, half = s.shape
    steps = times // 2
    args = [weights, x, s, c] + [a for pair in halo_taps for a in pair] + [bias, thr, *begun]
    grad = shape((steps, rows + 2, cols, half))
    res = shape((steps, rows, cols, half))
    return call(
        functools.partial(forward_kernel, two, bool(begun)),
        (grad, grad, res, res),
        [VMEM_SPEC] * len(args),
        16,
        "forward",
        [pltpu.VMEM((rows + (3 if two else 4), times * cols, weights.shape[0]), F32)],
        cost=24 << 20,
    )(*args)


def rows_of_grads(g_ref, t, h0, count):
    cols, half = g_ref.shape[2:]
    main, tail, padded = split_half(half)
    taps = [g_ref[t, pl.ds(h0 + 2 - dy, count)].reshape(count * cols, half) for dy in range(TAPS)]
    rest = jnp.zeros((count * cols, padded - TAPS * half), BF16)
    return jnp.concatenate([x[:, :main] for x in taps] + [x[:, main:] for x in taps] + [rest], axis=1)


def backward_own_kernel(w_ref, g_ref, y_ref):
    steps, rows2 = g_ref.shape[:2]
    rows = rows2 - 2
    for t in range(steps):
        grads = rows_of_grads(g_ref, t, 0, rows)
        y_ref[t] = dot(grads, w_ref[...], ((1,), (0,)))


def backward_own(weights, grads):
    steps, rows2, cols, _ = grads.shape
    out = shape((steps, (rows2 - 2) * cols, weights.shape[1]), F32)
    return call(backward_own_kernel, out, [VMEM_SPEC] * 2, 12, "backward_own", cost=6 << 20)(weights, grads)


def backward_kernel(w_ref, g_ref, y_ref, cot_ref, rk_ref, rs_ref, out_ref, res_ref):
    t = pl.program_id(0)
    _, rows, cols, ch = cot_ref.shape
    core = lax.axis_index("tm")
    edge = lax.broadcasted_iota(jnp.int32, (1, cols, 1), 1)
    block = 4
    for h0 in range(0, rows, block):
        total = dot(rows_of_grads(g_ref, t, h0, block), w_ref[...], ((1,), (0,)))
        total = (total + y_ref[t, h0 * cols : (h0 + block) * cols, :]).reshape(block, cols, -1)
        left, mid, right = (total[:, :, k * ch : (k + 1) * ch] for k in range(TAPS))
        left = jnp.where(edge == cols - 1, 0.0, pltpu.roll(left, cols - 1, 1))
        right = jnp.where(edge == 0, 0.0, pltpu.roll(right, 1, 1))
        out_ref[0, h0 : h0 + block] = cot_ref[t, h0 : h0 + block].astype(F32) + (left + mid + right)
        a = rk_ref[t, h0 : h0 + block].astype(F32)
        b = rs_ref[t, h0 : h0 + block].astype(F32)
        both = jnp.concatenate([jnp.where(core == 0, a, b), jnp.where(core == 0, b, a)], axis=2)
        res_ref[0, h0 : h0 + block] = both.astype(BF16)


def backward(weights, grads, y, cot, res_keep, res_arrived):
    block = pl.BlockSpec((1,) + cot.shape[1:], lambda t: (t, 0, 0, 0))
    return call(
        backward_kernel,
        (shape(cot.shape, F32), shape(cot.shape)),
        [VMEM_SPEC] * 6,
        16,
        "backward",
        grid=(cot.shape[0],),
        out_specs=(block, block),
    )(weights, grads, y, cot, res_keep, res_arrived)


def swap_cores(x):
    return lax.ppermute(x, "tm", [(0, 1), (1, 0)])


def fetch_halos(two, halos):
    if two:
        return [lax.ppermute(halos[0], "rows", [(0, 1), (1, 0)])]
    count = lax.axis_size("rows")
    head, tail = halos
    return [
        lax.ppermute(tail, "rows", [(i, i + 1) for i in range(count - 1)]),
        lax.ppermute(head, "rows", [(i + 1, i) for i in range(count - 1)]),
    ]


def on_device(spikes, cotangent, weight_codes, block_exponents, current_bias, threshold):
    two = lax.axis_size("rows") == 2
    spikes, cot = spikes[0], cotangent[0]
    w, send, *halos = prepare(two, weight_codes, block_exponents, spikes, cot)
    lanes = QUARTERS * w.shape[2]
    halos = fetch_halos(two, halos)
    taps = build_taps(spikes, cot, swap_cores(spikes), swap_cores(cot), lanes)
    taps, halos = lax.optimization_barrier((taps, halos))
    join, taps, first = fetch_weights(w, send, taps)
    halo_taps = [build_halo_taps(x, swap_cores(x), lanes) for x in halos]
    begun = [first(taps, halo_taps)] if first else []
    w, taps, halo_taps, begun = lax.optimization_barrier((w, taps, halo_taps, begun))
    weights = join(w)
    weights2 = swap_cores(weights)
    keep, send, res_keep, res_send = forward(two, weights, taps, halo_taps, current_bias, threshold, begun)
    arrived = swap_cores(send)
    res_arrived = swap_cores(res_send)
    y = backward_own(weights, keep)
    input_grad, residual = backward(weights2, arrived, y, cot, res_keep, res_arrived)
    return residual[None], input_grad[None]


def solution(mesh):
    return jax.shard_map(
        on_device,
        mesh=mesh,
        in_specs=(
            P(("groups", "dp"), "tm", "rows", None, None),
            P(("groups", "dp"), "tm", "rows", None, None),
            P(None, None, None, "dp"),
            P(None, None, None, "dp"),
            P(),
            P(),
        ),
        out_specs=(
            P(("groups", "dp"), "tm", "rows", None, None),
            P(("groups", "dp"), "tm", "rows", None, None),
        ),
        check_vma=False,
    )
```

```python
import functools

import jax
import jax.numpy as jnp
from jax import lax
from jax.experimental import pallas as pl
from jax.experimental.pallas import tpu as pltpu
from jax.sharding import PartitionSpec as P

MX_BLOCK = 32
TAPS = 3
F32 = jnp.float32
BF16 = jnp.bfloat16
VMEM_SPEC = pl.BlockSpec(memory_space=pltpu.VMEM)
HBM_SPEC = pl.BlockSpec(memory_space=pltpu.HBM)
QUARTERS = 4


def call(body, out_shape, in_specs, mib, name, scratch=(), grid=(), out_specs=None, cost=0):
    return pl.pallas_call(
        body,
        out_shape=out_shape,
        grid=grid,
        in_specs=in_specs,
        out_specs=out_specs or jax.tree.map(lambda _: VMEM_SPEC, out_shape),
        scratch_shapes=list(scratch),
        compiler_params=pltpu.CompilerParams(vmem_limit_bytes=mib << 20),
        cost_estimate=pl.CostEstimate(flops=0, transcendentals=0, bytes_accessed=cost) if cost else None,
        name=name,
    )


def in_hbm(x):
    return pltpu.with_memory_space_constraint(x, pltpu.HBM)


def shape(dims, dtype=BF16):
    return jax.ShapeDtypeStruct(dims, dtype)


def dot(a, b, dims):
    return lax.dot_general(a, b, (dims, ((), ())), preferred_element_type=F32)


def quarter_here():
    return lax.axis_index("groups") * 2 + lax.rem(lax.axis_index("rows"), 2)


def prepare_kernel(two, codes_hbm, exps_hbm, spikes_ref, cot_ref, *refs):
    w_ref, send_ref = refs[:2]
    halo_refs, (codes_ref, exps_ref, sems, code_sems) = refs[2:-4], refs[-4:]
    if two:
        halos = [(halo_refs[0], 1 - lax.axis_index("rows"))]
    else:
        halos = [(halo_refs[0], 0), (halo_refs[1], 1)]
    steps, rows = spikes_ref.shape[:2]
    scales = pltpu.make_async_copy(exps_hbm, exps_ref, code_sems.at[TAPS])
    codes = [pltpu.make_async_copy(codes_hbm.at[dy], codes_ref.at[dy], code_sems.at[dy]) for dy in range(TAPS)]
    scales.start()
    for copy in codes:
        copy.start()
    copies = []
    for n, (ref, end) in enumerate(halos):
        for t in range(steps):
            s = spikes_ref.at[t, pl.ds(end * (rows - 2), 2)]
            c = cot_ref.at[t, pl.ds(end * (rows - 1), 1)]
            copies.append(pltpu.make_async_copy(s, ref.at[t, pl.ds(0, 2)], sems.at[len(copies)]))
            copies.append(pltpu.make_async_copy(c, ref.at[t, pl.ds(2, 1)], sems.at[len(copies)]))
    for copy in copies:
        copy.start()
    outs, ins = codes_ref.shape[2:]
    blocks = exps_ref.shape[1]
    width = w_ref.shape[2]
    spread = lax.broadcasted_iota(jnp.int32, (blocks, ins), 1) // MX_BLOCK
    spread = (spread == lax.broadcasted_iota(jnp.int32, (blocks, ins), 0)).astype(F32).astype(BF16)
    scales.wait()
    every = []
    for n in range(TAPS * TAPS):
        scale = 1.0 / lax.shift_left(jnp.int32(1), -exps_ref[n // TAPS, :, n % TAPS, :]).astype(F32)
        every.append(dot(scale.astype(BF16), spread, ((0,), (0,))))
    for dy in range(TAPS):
        codes[dy].wait()
        parts = []
        for dx in range(TAPS):
            parts.append(codes_ref[dy, dx].astype(F32) * every[dy * TAPS + dx])
        parts.append(jnp.zeros((outs, QUARTERS * width - TAPS * ins), F32))
        tap = jnp.concatenate(parts, axis=1).astype(BF16)
        for q in range(QUARTERS):
            w_ref[q, dy * outs : (dy + 1) * outs, :] = tap[:, q * width : (q + 1) * width]
    q = quarter_here()
    send_ref[: TAPS * outs] = w_ref[q]
    send_ref[TAPS * outs :] = w_ref[QUARTERS - 1 - q]
    for copy in copies:
        copy.wait()


def prepare(two, weight_codes, block_exponents, spikes, cot):
    outs = weight_codes.shape[3]
    steps, rows, cols, ch = spikes.shape
    width = -(-TAPS * ch // (QUARTERS * 128)) * 128
    n_halo = 1 if two else 2
    out = (shape((QUARTERS, TAPS * outs, width)), shape((2 * TAPS * outs, width))) + (shape((steps, 3, cols, ch)),) * n_halo
    return call(
        functools.partial(prepare_kernel, two),
        out,
        [HBM_SPEC] * 4,
        16,
        "prepare",
        [
            pltpu.VMEM((TAPS, TAPS, outs, ch), jnp.int32),
            pltpu.VMEM((TAPS, block_exponents.shape[2], TAPS, outs), jnp.int32),
            pltpu.SemaphoreType.DMA((2 * steps * n_halo,)),
            pltpu.SemaphoreType.DMA((TAPS + 1,)),
        ],
        cost=2 << 20,
    )(*map(in_hbm, (weight_codes.transpose(0, 1, 3, 2), block_exponents.transpose(0, 2, 1, 3), spikes, cot)))


def put_taps(x_ref, x, s, t):
    cols, ch = x.shape
    edge = lax.broadcasted_iota(jnp.int32, (cols, 1), 0)
    before = jnp.where(edge == 0, 0.0, pltpu.roll(x, 1, 0))
    after = jnp.where(edge == cols - 1, 0.0, pltpu.roll(x, cols - 1, 0))
    pad = jnp.zeros((cols, x_ref.shape[2] - TAPS * ch), F32)
    taps = jnp.concatenate([before, x, after, pad], axis=1)
    x_ref[s, pl.ds(pl.multiple_of(t * cols, cols), cols), :] = taps.astype(BF16)


def half_of(x):
    half = x.shape[-1] // 2
    return jnp.where(lax.axis_index("tm") == 0, x[:, :half], x[:, half:])


def taps_kernel(spikes_ref, spikes2_ref, cot_ref, cot2_ref, x_ref, s_ref, c_ref):
    steps, rows = spikes_ref.shape[:2]
    for which, (s_in, c_in) in enumerate(((spikes_ref, cot_ref), (spikes2_ref, cot2_ref))):

        def body(n, carry, s_in=s_in, c_in=c_in, which=which):
            t, h = n // rows, n % rows
            x = s_in[t, h].astype(F32)
            put_taps(x_ref, x, h, which * steps + t)
            s_ref[h, which * steps + t] = half_of(x).astype(BF16)
            c_ref[h, which * steps + t] = half_of(c_in[t, h].astype(F32)).astype(BF16)
            return carry

        lax.fori_loop(0, steps * rows, body, 0)


def build_taps(spikes, cot, spikes2, cot2, lanes):
    steps, rows, cols, ch = spikes.shape
    half = shape((rows, 2 * steps, cols, ch // 2))
    out = (shape((rows, 2 * steps * cols, lanes)), half, half)
    return call(taps_kernel, out, [VMEM_SPEC] * 4, 16, "taps", cost=18 << 20)(spikes, spikes2, cot, cot2)


def halo_taps_kernel(halo_ref, halo2_ref, x_ref, c_ref):
    steps = halo_ref.shape[0]
    for which, ref in enumerate((halo_ref, halo2_ref)):

        def body(t, carry, ref=ref, which=which):
            for k in range(2):
                put_taps(x_ref, ref[t, k].astype(F32), k, which * steps + t)
            c_ref[which * steps + t] = half_of(ref[t, 2].astype(F32)).astype(BF16)
            return carry

        lax.fori_loop(0, steps, body, 0)


def build_halo_taps(halo, halo2, lanes):
    steps, _, cols, ch = halo.shape
    out = (shape((2, 2 * steps * cols, lanes)), shape((2 * steps, cols, ch // 2)))
    return call(halo_taps_kernel, out, [VMEM_SPEC] * 2, 16, "halo_taps", cost=2 << 20)(halo, halo2)


def split_half(half):
    main = half // 128 * 128
    return main, half - main, TAPS * main + -(-TAPS * (half - main) // 128) * 128


def put_rows(out_ref, part, lane, pos):
    outs, width = part.shape[0] // TAPS, part.shape[1]
    main, tail, _ = split_half(2 * outs)
    at = pl.ds(pl.multiple_of(lane * width, width), width)
    for dy in range(TAPS):
        for o in range(0, outs, 16):
            c = pos * outs + o
            to = dy * main + c if c < main else TAPS * main + dy * tail + c - main
            out_ref[to : to + 16, at] = part[dy * outs + o : dy * outs + o + 16, :]


def put_shards(out_ref, own_parts, rounds):
    z, core = lax.axis_index("dp"), lax.axis_index("tm")
    own = core == z // 2

    def put_all(parts, pos):
        for part, lane in parts:
            put_rows(out_ref, part, lane, pos)

    for even in range(2):

        @pl.when(lax.rem(z, 2) == even)
        def _():
            pl.when(own)(lambda: put_all(own_parts, even))
            pl.when(jnp.logical_not(own))(lambda: put_all(rounds[0], even))
            put_all(rounds[1], 1 - even)

    used = 2 * rounds[0][0][0].shape[0]
    out_ref[used:, :] = jnp.zeros((out_ref.shape[0] - used, out_ref.shape[1]), BF16)


def lanes_here():
    q = quarter_here()
    return (q, QUARTERS - 1 - q), (jnp.bitwise_xor(q, 1), jnp.bitwise_xor(q, 2))


def join_kernel(w_ref, first_ref, second_ref, x_ref, y_ref, out_ref):
    size = w_ref.shape[1]
    halves = [pl.ds(k * size, size) for k in range(2)]
    here, there = lanes_here()
    rounds = []
    for k, ref in enumerate((first_ref, second_ref)):
        parts = ref.at[halves[0]], ref.at[halves[1]], x_ref.at[halves[k]], y_ref.at[halves[k]]
        rounds.append(list(zip(parts, here + there)))
    put_shards(out_ref, [(w_ref.at[n], n) for n in range(QUARTERS)], rounds)


def partial_kernel(w_ref, first_ref, second_ref, x_ref, halo_ref, p_ref, wh_ref):
    size, width = w_ref.shape[1:]
    halves = [pl.ds(k * size, size) for k in range(2)]
    here, _ = lanes_here()
    rounds = [[(ref.at[halves[n]], n) for n in range(2)] for ref in (first_ref, second_ref)]
    put_shards(wh_ref, [(w_ref.at[here[n]], n) for n in range(2)], rounds)
    for x, h, strip in strips(x_ref, halo_ref):
        p_ref[pl.ds(strip, 2)] = dot(take_lanes(x, h, here, width), wh_ref[...], ((1,), (1,))).reshape(2, -1, wh_ref.shape[0])


def take_lanes(x, h, lanes, width):
    parts = [x[pl.ds(h, 2), :, pl.ds(pl.multiple_of(n * width, width), width)] for n in lanes]
    return jnp.concatenate([part.reshape(-1, width) for part in parts], axis=1)


def strips(x_ref, halo_ref):
    rows = x_ref.shape[0]
    flip = lax.axis_index("rows") == 1
    todo = []
    for i in range(0, rows, 2):
        h = jnp.where(flip, rows - 2 - i, i)
        todo.append((x_ref, h, jnp.where(flip, h + 2, h + 1)))
    return todo + [(halo_ref, 0, jnp.where(flip, 0, rows + 1))]


def partial_currents(two, w, rounds, taps, halo_taps):
    x = taps[0]
    main, tail, padded = split_half(2 * w.shape[1] // TAPS)
    out = shape((x.shape[0] + 3, x.shape[1], padded), F32)
    scratch = [pltpu.VMEM((padded, 2 * w.shape[2]), BF16)]
    return call(partial_kernel, out, [VMEM_SPEC] * 5, 12, "partial", scratch)(w, *rounds, x, halo_taps[0][0])


def fetch_weights(w, send, after):
    count = lax.axis_size("dp")
    n_rows = lax.axis_size("rows")
    h = count // 2
    outs = w.shape[1] // TAPS
    lanes = QUARTERS * w.shape[2]

    def pairs(k):
        todo = []
        for z in range(count):
            for c in range(2):
                s = c * h + (z + k) % h
                todo.append((s * 2 + z // h, z * 2 + c))
        return todo

    main, tail, padded = split_half(h * outs)
    if h == 2 and outs % 16 == 0 and n_rows % 2 == 0 and lax.axis_size("groups") == 2:
        moved = [[(a, b) for a, b in pairs(k) if a != b] for k in range(h)]
        rounds = [lax.ppermute(send, ("dp", "tm"), moved[k]) for k in range(h)]
        rounds, after = lax.optimization_barrier((rounds, after))
        first = functools.partial(partial_currents, True, w, rounds) if n_rows == 2 else None
        both = jnp.concatenate([r[: TAPS * outs] for r in rounds])
        x = lax.ppermute(both, "rows", [(r, r ^ 1) for r in range(n_rows)])
        y = lax.ppermute(both, "groups", [(0, 1), (1, 0)])
        return lambda w: call(join_kernel, shape((padded, lanes)), [VMEM_SPEC] * 5, 8, "join")(w, *rounds, x, y), after, first
    w = w.reshape(QUARTERS, TAPS, outs, -1).transpose(1, 2, 0, 3).reshape(TAPS, outs, lanes)
    stack = jnp.stack([lax.ppermute(w, ("dp", "tm"), pairs(k)) for k in range(h)], axis=1)
    stack = jnp.roll(stack, lax.axis_index("dp") % h, axis=1).reshape(TAPS, h * outs, lanes)
    rest = jnp.zeros((padded - TAPS * h * outs, lanes), BF16)
    joined = jnp.concatenate([stack[:, :main].reshape(-1, lanes), stack[:, main:].reshape(-1, lanes), rest])
    return lambda w: joined, after, None


def forward_kernel(two, started, w_ref, x_ref, s_ref, c_ref, *refs):
    if two:
        halos = [refs[:2]]
    else:
        halos = [refs[:2], refs[2:4]]
    bias_ref, thr_ref, *begun, gk_ref, gs_ref, rk_ref, rs_ref, p_ref = refs[2 * len(halos) :]
    core, row = lax.axis_index("tm"), lax.axis_index("rows")
    rows, times, cols, half = s_ref.shape
    lanes = x_ref.shape[2]
    steps = times // 2
    main, tail, _ = split_half(half)
    chunk = cols * tail // main

    def half_row(ref):
        x = ref[...].reshape(1, 2 * half)
        return jnp.where(core == 0, x[:, :half], x[:, half:])

    thr = half_row(thr_ref)
    shift = half_row(bias_ref) - thr
    at_of = [lax.rem(core + part, 2) * steps + tl for part in range(2) for tl in range(steps)]

    if started:
        _, there = lanes_here()
        width = lanes // QUARTERS
        w_there = jnp.concatenate([w_ref[:, pl.ds(pl.multiple_of(n * width, width), width)] for n in there], axis=1)

    def currents(x, h, strip):
        if started:
            p = dot(take_lanes(x, h, there, width), w_there, ((1,), (1,)))
            p_ref[pl.ds(strip, 2)] = begun[0][pl.ds(strip, 2)] + p.reshape(2, times * cols, -1)
        else:
            p = dot(x[pl.ds(h, 2)].reshape(-1, lanes), w_ref[...], ((1,), (1,)))
            p_ref[pl.ds(strip, 2)] = p.reshape(2, times * cols, -1)

    def scan(strip, cot, spike, g, h, keep=None):
        for w0 in range(0, cols, chunk):
            for lo, width, first in ((0, main, 0), (main, tail, TAPS * main)):
                th = thr[:, lo : lo + width]
                half_th = 0.5 * th
                sh = shift[:, lo : lo + width]
                state = jnp.zeros((chunk, width), F32)
                tanhs = []
                for t in range(times):
                    at = pl.ds(pl.multiple_of(at_of[t] * cols + w0, chunk), chunk)
                    now = sh
                    for dy in range(TAPS):
                        now = now + p_ref[strip + dy, at, first + dy * width : first + (dy + 1) * width]
                    y = state + now
                    tanh = jnp.tanh(y)
                    state = (y + half_th) - half_th * tanh
                    tanhs.append(tanh)
                adjoint = jnp.zeros((chunk, width), F32)
                grads, res = [None] * times, [None] * times
                for t in reversed(range(times)):
                    here = slice(w0, w0 + chunk), slice(lo, lo + width)
                    slope = 0.5 - 0.5 * (tanhs[t] * tanhs[t])
                    up = cot(at_of[t], here).astype(F32)
                    adjoint = adjoint + slope * (up - th * adjoint)
                    out = adjoint if keep is None else adjoint * keep
                    grads[t] = out.astype(BF16)
                    if h is not None:
                        fired = 0.5 + 0.5 * tanhs[t]
                        res[t] = (fired + spike(at_of[t], here).astype(F32)).astype(BF16)
                mine = core == 0
                if lo == 0:
                    put = slice(w0, w0 + chunk), slice(None)
                else:
                    put = slice(cols, cols + chunk), slice(w0 // chunk * tail, (w0 // chunk + 1) * tail)
                for tl in range(steps):
                    a, b = grads[tl], grads[steps + tl]
                    gk_ref[tl, g, put[0], put[1]] = jnp.where(mine, a, b)
                    gs_ref[tl, g, put[0], put[1]] = jnp.where(mine, b, a)
                    if h is not None:
                        a, b = res[tl], res[steps + tl]
                        rk_ref[tl, h, put[0], put[1]] = jnp.where(mine, a, b)
                        rs_ref[tl, h, put[0], put[1]] = jnp.where(mine, b, a)

    def scan_own(h, strip):
        scan(
            strip,
            lambda at, here: c_ref[h, at, here[0], here[1]],
            lambda at, here: s_ref[h, at, here[0], here[1]],
            h + 1,
            h,
        )

    def scan_halo(n, strip, g, keep=None):
        scan(strip, lambda at, here: halos[n][1][at, here[0], here[1]], None, g, None, keep)

    if two:
        flip = row == 1
        edge_strip = jnp.where(flip, rows + 2, 0)
        edge = jnp.where(flip, rows + 1, 0)
        p_ref[edge_strip] = jnp.zeros(p_ref.shape[1:], F32)
        for ref in (gk_ref, gs_ref):
            for tl in range(steps):
                ref[tl, edge] = jnp.zeros(ref.shape[2:], BF16)

        def scan_at(j):
            if j == rows:
                scan_halo(0, jnp.where(flip, 0, rows), jnp.where(flip, 0, rows + 1))
            elif 0 <= j < rows:
                h = jnp.where(flip, rows - 1 - j, j)
                scan_own(h, jnp.where(flip, h + 1, h))

        done = 0
        for i, (x, h, strip) in enumerate(strips(x_ref, halos[0][0])):
            currents(x, h, strip)
            while done <= 2 * i - 2:
                scan_at(done)
                done += 1
        while done <= rows:
            scan_at(done)
            done += 1
    else:
        last = lax.axis_size("rows") - 1
        currents(halos[0][0], 0, 0)
        currents(halos[1][0], 0, rows + 2)

        def pair(i, carry):
            currents(x_ref, 2 * i, 2 * i + 2)
            return carry

        lax.fori_loop(0, rows // 2, pair, 0)

        def one(h, carry):
            scan_own(h, h + 1)
            return carry

        lax.fori_loop(0, rows, one, 0)
        scan_halo(0, 0, 0, jnp.where(row == 0, 0.0, 1.0))
        scan_halo(1, rows + 1, rows + 1, jnp.where(row == last, 0.0, 1.0))


def forward(two, weights, taps, halo_taps, bias, thr, begun=()):
    x, s, c = taps
    rows, times, cols, half = s.shape
    steps = times // 2
    args = [weights, x, s, c] + [a for pair in halo_taps for a in pair] + [bias, thr, *begun]
    main, tail, _ = split_half(half)
    grad = shape((steps, rows + 2, cols + cols * tail // main, main))
    res = shape((steps, rows, cols + cols * tail // main, main))
    return call(
        functools.partial(forward_kernel, two, bool(begun)),
        (grad, grad, res, res),
        [VMEM_SPEC] * len(args),
        16,
        "forward",
        [pltpu.VMEM((rows + (3 if two else 4), times * cols, weights.shape[0]), F32)],
        cost=24 << 20,
    )(*args)


def unpack(x, cols):
    main = x.shape[2]
    chunk = x.shape[1] - cols
    tail = main * chunk // cols
    parts = [x[:, cols:, k * tail : (k + 1) * tail] for k in range(cols // chunk)]
    return x[:, :cols], jnp.concatenate(parts, axis=1)


def rows_of_grads(g_ref, t, h0, count, cols, padded):
    taps = [unpack(g_ref[t, pl.ds(h0 + 2 - dy, count)], cols) for dy in range(TAPS)]
    mains, tails = ([x[k].reshape(count * cols, -1) for x in taps] for k in range(2))
    rest = jnp.zeros((count * cols, padded - sum(x.shape[1] for x in mains + tails)), BF16)
    return jnp.concatenate(mains + tails + [rest], axis=1)


def backward_own_kernel(w_ref, g_ref, y_ref):
    steps, rows2 = g_ref.shape[:2]
    rows = rows2 - 2
    for t in range(steps):
        grads = rows_of_grads(g_ref, t, 0, rows, y_ref.shape[1] // rows, w_ref.shape[0])
        y_ref[t] = dot(grads, w_ref[...], ((1,), (0,)))


def backward_own(weights, grads, cols):
    steps, rows2 = grads.shape[:2]
    out = shape((steps, (rows2 - 2) * cols, weights.shape[1]), F32)
    return call(backward_own_kernel, out, [VMEM_SPEC] * 2, 12, "backward_own", cost=6 << 20)(weights, grads)


def backward_kernel(w_ref, g_ref, y_ref, cot_ref, rk_ref, rs_ref, out_hbm, res_hbm, out_ref, res_ref, sems):
    steps, rows, cols, ch = cot_ref.shape
    core = lax.axis_index("tm")
    edge = lax.broadcasted_iota(jnp.int32, (1, cols, 1), 1)
    block = 4
    copies = []
    for t in range(steps):
        for h0 in range(0, rows, block):
            total = dot(rows_of_grads(g_ref, t, h0, block, cols, w_ref.shape[0]), w_ref[...], ((1,), (0,)))
            total = (total + y_ref[t, h0 * cols : (h0 + block) * cols, :]).reshape(block, cols, -1)
            left, mid, right = (total[:, :, k * ch : (k + 1) * ch] for k in range(TAPS))
            left = jnp.where(edge == cols - 1, 0.0, pltpu.roll(left, cols - 1, 1))
            right = jnp.where(edge == 0, 0.0, pltpu.roll(right, 1, 1))
            here = t, slice(h0, h0 + block)
            out_ref[here] = cot_ref[here].astype(F32) + (left + mid + right)
            a, b = (jnp.concatenate(unpack(ref[here].astype(F32), cols), axis=2) for ref in (rk_ref, rs_ref))
            both = jnp.concatenate([jnp.where(core == 0, a, b), jnp.where(core == 0, b, a)], axis=2)
            res_ref[here] = both.astype(BF16)
            for n, (ref, hbm) in enumerate(((out_ref, out_hbm), (res_ref, res_hbm))):
                window = t, pl.ds(h0, block)
                copies.append(pltpu.make_async_copy(ref.at[window], hbm.at[window], sems.at[len(copies)]))
                copies[-1].start()
    for copy in copies:
        copy.wait()


def backward(weights, grads, y, cot, res_keep, res_arrived):
    steps, rows = cot.shape[:2]
    return call(
        backward_kernel,
        (shape(cot.shape, F32), shape(cot.shape)),
        [VMEM_SPEC] * 6,
        24,
        "backward",
        [
            pltpu.VMEM(cot.shape, F32),
            pltpu.VMEM(cot.shape, BF16),
            pltpu.SemaphoreType.DMA((2 * steps * (rows // 4),)),
        ],
        out_specs=(pl.BlockSpec(memory_space=pltpu.HBM),) * 2,
    )(weights, grads, y, cot, res_keep, res_arrived)


def swap_cores(x):
    return lax.ppermute(x, "tm", [(0, 1), (1, 0)])


def fetch_halos(two, halos):
    if two:
        return [lax.ppermute(halos[0], "rows", [(0, 1), (1, 0)])]
    count = lax.axis_size("rows")
    head, tail = halos
    return [
        lax.ppermute(tail, "rows", [(i, i + 1) for i in range(count - 1)]),
        lax.ppermute(head, "rows", [(i + 1, i) for i in range(count - 1)]),
    ]


def on_device(spikes, cotangent, weight_codes, block_exponents, current_bias, threshold):
    two = lax.axis_size("rows") == 2
    spikes, cot = spikes[0], cotangent[0]
    w, send, *halos = prepare(two, weight_codes, block_exponents, spikes, cot)
    lanes = QUARTERS * w.shape[2]
    halos = fetch_halos(two, halos)
    taps = build_taps(spikes, cot, swap_cores(spikes), swap_cores(cot), lanes)
    taps, halos = lax.optimization_barrier((taps, halos))
    join, taps, first = fetch_weights(w, send, taps)
    halo_taps = [build_halo_taps(x, swap_cores(x), lanes) for x in halos]
    begun = [first(taps, halo_taps)] if first else []
    w, taps, halo_taps, begun = lax.optimization_barrier((w, taps, halo_taps, begun))
    weights = join(w)
    weights2 = swap_cores(weights)
    keep, send, res_keep, res_send = forward(two, weights, taps, halo_taps, current_bias, threshold, begun)
    arrived = swap_cores(send)
    res_arrived = swap_cores(res_send)
    y = backward_own(weights, keep, cot.shape[2])
    input_grad, residual = backward(weights2, arrived, y, cot, res_keep, res_arrived)
    return residual[None], input_grad[None]


def solution(mesh):
    return jax.shard_map(
        on_device,
        mesh=mesh,
        in_specs=(
            P(("groups", "dp"), "tm", "rows", None, None),
            P(("groups", "dp"), "tm", "rows", None, None),
            P(None, None, None, "dp"),
            P(None, None, None, "dp"),
            P(),
            P(),
        ),
        out_specs=(
            P(("groups", "dp"), "tm", "rows", None, None),
            P(("groups", "dp"), "tm", "rows", None, None),
        ),
        check_vma=False,
    )
```

```python
import functools

import jax
import jax.numpy as jnp
from jax import lax
from jax.experimental import pallas as pl
from jax.experimental.pallas import tpu as pltpu
from jax.sharding import PartitionSpec as P

MX_BLOCK = 32
TAPS = 3
F32 = jnp.float32
BF16 = jnp.bfloat16
VMEM_SPEC = pl.BlockSpec(memory_space=pltpu.VMEM)
HBM_SPEC = pl.BlockSpec(memory_space=pltpu.HBM)
QUARTERS = 4


def call(body, out_shape, in_specs, mib, name, scratch=(), grid=(), out_specs=None, cost=0):
    return pl.pallas_call(
        body,
        out_shape=out_shape,
        grid=grid,
        in_specs=in_specs,
        out_specs=out_specs or jax.tree.map(lambda _: VMEM_SPEC, out_shape),
        scratch_shapes=list(scratch),
        compiler_params=pltpu.CompilerParams(vmem_limit_bytes=mib << 20),
        cost_estimate=pl.CostEstimate(flops=0, transcendentals=0, bytes_accessed=cost) if cost else None,
        name=name,
    )


def in_hbm(x):
    return pltpu.with_memory_space_constraint(x, pltpu.HBM)


def shape(dims, dtype=BF16):
    return jax.ShapeDtypeStruct(dims, dtype)


def dot(a, b, dims):
    return lax.dot_general(a, b, (dims, ((), ())), preferred_element_type=F32)


def quarter_here():
    return lax.axis_index("groups") * 2 + lax.rem(lax.axis_index("rows"), 2)


def prepare_kernel(two, codes_hbm, exps_hbm, spikes_ref, cot_ref, *refs):
    w_ref, send_ref = refs[:2]
    halo_refs, (codes_ref, exps_ref, sems, code_sems) = refs[2:-4], refs[-4:]
    if two:
        halos = [(halo_refs[0], 1 - lax.axis_index("rows"))]
    else:
        halos = [(halo_refs[0], 0), (halo_refs[1], 1)]
    steps, rows = spikes_ref.shape[:2]
    scales = pltpu.make_async_copy(exps_hbm, exps_ref, code_sems.at[TAPS])
    codes = [pltpu.make_async_copy(codes_hbm.at[dy], codes_ref.at[dy], code_sems.at[dy]) for dy in range(TAPS)]
    scales.start()
    for copy in codes:
        copy.start()
    copies = []
    for n, (ref, end) in enumerate(halos):
        for t in range(steps):
            s = spikes_ref.at[t, pl.ds(end * (rows - 2), 2)]
            c = cot_ref.at[t, pl.ds(end * (rows - 1), 1)]
            copies.append(pltpu.make_async_copy(s, ref.at[t, pl.ds(0, 2)], sems.at[len(copies)]))
            copies.append(pltpu.make_async_copy(c, ref.at[t, pl.ds(2, 1)], sems.at[len(copies)]))
    for copy in copies:
        copy.start()
    outs, ins = codes_ref.shape[2:]
    blocks = exps_ref.shape[1]
    width = w_ref.shape[2]
    spread = lax.broadcasted_iota(jnp.int32, (blocks, ins), 1) // MX_BLOCK
    spread = (spread == lax.broadcasted_iota(jnp.int32, (blocks, ins), 0)).astype(F32).astype(BF16)
    scales.wait()
    every = []
    for n in range(TAPS * TAPS):
        scale = 1.0 / lax.shift_left(jnp.int32(1), -exps_ref[n // TAPS, :, n % TAPS, :]).astype(F32)
        every.append(dot(scale.astype(BF16), spread, ((0,), (0,))))
    for dy in range(TAPS):
        codes[dy].wait()
        parts = []
        for dx in range(TAPS):
            parts.append(codes_ref[dy, dx].astype(F32) * every[dy * TAPS + dx])
        parts.append(jnp.zeros((outs, QUARTERS * width - TAPS * ins), F32))
        tap = jnp.concatenate(parts, axis=1).astype(BF16)
        for q in range(QUARTERS):
            w_ref[q, dy * outs : (dy + 1) * outs, :] = tap[:, q * width : (q + 1) * width]
    q = quarter_here()
    send_ref[: TAPS * outs] = w_ref[q]
    send_ref[TAPS * outs :] = w_ref[QUARTERS - 1 - q]
    for copy in copies:
        copy.wait()


def prepare(two, weight_codes, block_exponents, spikes, cot):
    outs = weight_codes.shape[3]
    steps, rows, cols, ch = spikes.shape
    width = -(-TAPS * ch // (QUARTERS * 128)) * 128
    n_halo = 1 if two else 2
    out = (shape((QUARTERS, TAPS * outs, width)), shape((2 * TAPS * outs, width))) + (shape((steps, 3, cols, ch)),) * n_halo
    return call(
        functools.partial(prepare_kernel, two),
        out,
        [HBM_SPEC] * 4,
        16,
        "prepare",
        [
            pltpu.VMEM((TAPS, TAPS, outs, ch), jnp.int32),
            pltpu.VMEM((TAPS, block_exponents.shape[2], TAPS, outs), jnp.int32),
            pltpu.SemaphoreType.DMA((2 * steps * n_halo,)),
            pltpu.SemaphoreType.DMA((TAPS + 1,)),
        ],
        cost=2 << 20,
    )(*map(in_hbm, (weight_codes.transpose(0, 1, 3, 2), block_exponents.transpose(0, 2, 1, 3), spikes, cot)))


def put_taps(x_ref, x, s, t):
    cols, ch = x.shape
    edge = lax.broadcasted_iota(jnp.int32, (cols, 1), 0)
    before = jnp.where(edge == 0, 0.0, pltpu.roll(x, 1, 0))
    after = jnp.where(edge == cols - 1, 0.0, pltpu.roll(x, cols - 1, 0))
    pad = jnp.zeros((cols, x_ref.shape[2] - TAPS * ch), F32)
    taps = jnp.concatenate([before, x, after, pad], axis=1)
    x_ref[s, pl.ds(pl.multiple_of(t * cols, cols), cols), :] = taps.astype(BF16)


def half_of(x):
    half = x.shape[-1] // 2
    return jnp.where(lax.axis_index("tm") == 0, x[:, :half], x[:, half:])


def taps_kernel(spikes_ref, spikes2_ref, cot_ref, cot2_ref, x_ref, s_ref, c_ref):
    steps, rows = spikes_ref.shape[:2]
    for which, (s_in, c_in) in enumerate(((spikes_ref, cot_ref), (spikes2_ref, cot2_ref))):

        def body(n, carry, s_in=s_in, c_in=c_in, which=which):
            t, h = n // rows, n % rows
            x = s_in[t, h].astype(F32)
            put_taps(x_ref, x, h, which * steps + t)
            s_ref[h, which * steps + t] = half_of(x).astype(BF16)
            c_ref[h, which * steps + t] = half_of(c_in[t, h].astype(F32)).astype(BF16)
            return carry

        lax.fori_loop(0, steps * rows, body, 0)


def build_taps(spikes, cot, spikes2, cot2, lanes):
    steps, rows, cols, ch = spikes.shape
    half = shape((rows, 2 * steps, cols, ch // 2))
    out = (shape((rows, 2 * steps * cols, lanes)), half, half)
    return call(taps_kernel, out, [VMEM_SPEC] * 4, 16, "taps", cost=18 << 20)(spikes, spikes2, cot, cot2)


def halo_taps_kernel(halo_ref, halo2_ref, x_ref, c_ref):
    steps = halo_ref.shape[0]
    for which, ref in enumerate((halo_ref, halo2_ref)):

        def body(t, carry, ref=ref, which=which):
            for k in range(2):
                put_taps(x_ref, ref[t, k].astype(F32), k, which * steps + t)
            c_ref[which * steps + t] = half_of(ref[t, 2].astype(F32)).astype(BF16)
            return carry

        lax.fori_loop(0, steps, body, 0)


def build_halo_taps(halo, halo2, lanes):
    steps, _, cols, ch = halo.shape
    out = (shape((2, 2 * steps * cols, lanes)), shape((2 * steps, cols, ch // 2)))
    return call(halo_taps_kernel, out, [VMEM_SPEC] * 2, 16, "halo_taps", cost=2 << 20)(halo, halo2)


def split_half(half):
    main = half // 128 * 128
    return main, half - main, TAPS * main + -(-TAPS * (half - main) // 128) * 128


def put_rows(out_ref, part, lane, pos):
    outs, width = part.shape[0] // TAPS, part.shape[1]
    main, tail, _ = split_half(2 * outs)
    at = pl.ds(pl.multiple_of(lane * width, width), width)
    for dy in range(TAPS):
        for o in range(0, outs, 16):
            c = pos * outs + o
            to = dy * main + c if c < main else TAPS * main + dy * tail + c - main
            out_ref[to : to + 16, at] = part[dy * outs + o : dy * outs + o + 16, :]


def put_shards(out_ref, own_parts, rounds):
    z, core = lax.axis_index("dp"), lax.axis_index("tm")
    own = core == z // 2

    def put_all(parts, pos):
        for part, lane in parts:
            put_rows(out_ref, part, lane, pos)

    for even in range(2):

        @pl.when(lax.rem(z, 2) == even)
        def _():
            pl.when(own)(lambda: put_all(own_parts, even))
            pl.when(jnp.logical_not(own))(lambda: put_all(rounds[0], even))
            put_all(rounds[1], 1 - even)

    used = 2 * rounds[0][0][0].shape[0]
    out_ref[used:, :] = jnp.zeros((out_ref.shape[0] - used, out_ref.shape[1]), BF16)


def lanes_here():
    q = quarter_here()
    return (q, QUARTERS - 1 - q), (jnp.bitwise_xor(q, 1), jnp.bitwise_xor(q, 2))


def join_kernel(w_ref, first_ref, second_ref, x_ref, y_ref, out_ref):
    size = w_ref.shape[1]
    halves = [pl.ds(k * size, size) for k in range(2)]
    here, there = lanes_here()
    rounds = []
    for k, ref in enumerate((first_ref, second_ref)):
        parts = ref.at[halves[0]], ref.at[halves[1]], x_ref.at[halves[k]], y_ref.at[halves[k]]
        rounds.append(list(zip(parts, here + there)))
    put_shards(out_ref, [(w_ref.at[n], n) for n in range(QUARTERS)], rounds)


def partial_kernel(w_ref, first_ref, second_ref, x_ref, halo_ref, p_ref, wh_ref):
    size, width = w_ref.shape[1:]
    halves = [pl.ds(k * size, size) for k in range(2)]
    here, _ = lanes_here()
    rounds = [[(ref.at[halves[n]], n) for n in range(2)] for ref in (first_ref, second_ref)]
    put_shards(wh_ref, [(w_ref.at[here[n]], n) for n in range(2)], rounds)
    for x, h, strip in strips(x_ref, halo_ref):
        p_ref[pl.ds(strip, 2)] = dot(take_lanes(x, h, here, width), wh_ref[...], ((1,), (1,))).reshape(2, -1, wh_ref.shape[0])


def take_lanes(x, h, lanes, width):
    parts = [x[pl.ds(h, 2), :, pl.ds(pl.multiple_of(n * width, width), width)] for n in lanes]
    return jnp.concatenate([part.reshape(-1, width) for part in parts], axis=1)


def strips(x_ref, halo_ref):
    rows = x_ref.shape[0]
    flip = lax.axis_index("rows") == 1
    todo = []
    for i in range(0, rows, 2):
        h = jnp.where(flip, rows - 2 - i, i)
        todo.append((x_ref, h, jnp.where(flip, h + 2, h + 1)))
    return todo + [(halo_ref, 0, jnp.where(flip, 0, rows + 1))]


def partial_currents(two, w, rounds, taps, halo_taps):
    x = taps[0]
    main, tail, padded = split_half(2 * w.shape[1] // TAPS)
    out = shape((x.shape[0] + 3, x.shape[1], padded), F32)
    scratch = [pltpu.VMEM((padded, 2 * w.shape[2]), BF16)]
    return call(partial_kernel, out, [VMEM_SPEC] * 5, 12, "partial", scratch)(w, *rounds, x, halo_taps[0][0])


def fetch_weights(w, send, after):
    count = lax.axis_size("dp")
    n_rows = lax.axis_size("rows")
    h = count // 2
    outs = w.shape[1] // TAPS
    lanes = QUARTERS * w.shape[2]

    def pairs(k):
        todo = []
        for z in range(count):
            for c in range(2):
                s = c * h + (z + k) % h
                todo.append((s * 2 + z // h, z * 2 + c))
        return todo

    main, tail, padded = split_half(h * outs)
    if h == 2 and outs % 16 == 0 and n_rows % 2 == 0 and lax.axis_size("groups") == 2:
        moved = [[(a, b) for a, b in pairs(k) if a != b] for k in range(h)]
        rounds = [lax.ppermute(send, ("dp", "tm"), moved[k]) for k in range(h)]
        rounds, after = lax.optimization_barrier((rounds, after))
        first = functools.partial(partial_currents, True, w, rounds) if n_rows == 2 else None
        both = jnp.concatenate([r[: TAPS * outs] for r in rounds])
        x = lax.ppermute(both, "rows", [(r, r ^ 1) for r in range(n_rows)])
        y = lax.ppermute(both, "groups", [(0, 1), (1, 0)])
        return lambda w: call(join_kernel, shape((padded, lanes)), [VMEM_SPEC] * 5, 8, "join")(w, *rounds, x, y), after, first
    w = w.reshape(QUARTERS, TAPS, outs, -1).transpose(1, 2, 0, 3).reshape(TAPS, outs, lanes)
    stack = jnp.stack([lax.ppermute(w, ("dp", "tm"), pairs(k)) for k in range(h)], axis=1)
    stack = jnp.roll(stack, lax.axis_index("dp") % h, axis=1).reshape(TAPS, h * outs, lanes)
    rest = jnp.zeros((padded - TAPS * h * outs, lanes), BF16)
    joined = jnp.concatenate([stack[:, :main].reshape(-1, lanes), stack[:, main:].reshape(-1, lanes), rest])
    return lambda w: joined, after, None


def forward_kernel(two, started, w_ref, x_ref, s_ref, c_ref, *refs):
    if two:
        halos = [refs[:2]]
    else:
        halos = [refs[:2], refs[2:4]]
    bias_ref, thr_ref, *begun, gk_ref, gs_ref, rk_ref, rs_ref, p_ref = refs[2 * len(halos) :]
    core, row = lax.axis_index("tm"), lax.axis_index("rows")
    rows, times = s_ref.shape[:2]
    cols, half = x_ref.shape[1] // times, bias_ref.shape[0] // 2
    lanes = x_ref.shape[2]
    steps = times // 2
    main, tail, _ = split_half(half)
    chunk = cols * tail // main

    def half_row(ref):
        x = ref[...].reshape(1, 2 * half)
        return jnp.where(core == 0, x[:, :half], x[:, half:])

    thr = half_row(thr_ref)
    shift = half_row(bias_ref) - thr
    at_of = [lax.rem(core + part, 2) * steps + tl for part in range(2) for tl in range(steps)]

    if started:
        _, there = lanes_here()
        width = lanes // QUARTERS
        w_there = jnp.concatenate([w_ref[:, pl.ds(pl.multiple_of(n * width, width), width)] for n in there], axis=1)

    def currents(x, h, strip):
        if started:
            p = dot(take_lanes(x, h, there, width), w_there, ((1,), (1,)))
            p_ref[pl.ds(strip, 2)] = begun[0][pl.ds(strip, 2)] + p.reshape(2, times * cols, -1)
        else:
            p = dot(x[pl.ds(h, 2)].reshape(-1, lanes), w_ref[...], ((1,), (1,)))
            p_ref[pl.ds(strip, 2)] = p.reshape(2, times * cols, -1)

    def scan(strip, cot, spike, g, h, keep=None):
        def row_of(t, w0):
            return pl.ds(pl.multiple_of(at_of[t] * cols + w0, chunk), chunk)

        def below(t, dy, w0):
            return p_ref[strip + dy, row_of(t, w0), dy * main : (dy + 1) * main]

        def beyond(t, dy, _):
            first = TAPS * main + dy * tail
            parts = [p_ref[strip + dy, row_of(t, w0), first : first + tail] for w0 in range(0, cols, chunk)]
            return jnp.concatenate(parts, axis=1)

        def packed(read, at, w0):
            if w0 < cols:
                return read(at, slice(w0, w0 + chunk), slice(0, main))
            parts = [read(at, slice(w, w + chunk), slice(main, half)) for w in range(0, cols, chunk)]
            return jnp.concatenate(parts, axis=1)

        jobs = [(w0, below, thr[:, :main], shift[:, :main]) for w0 in range(0, cols, chunk)]
        spread = [jnp.concatenate([v[:, main:]] * (cols // chunk), axis=1) for v in (thr, shift)]
        for w0, part, th, sh in jobs + [(cols, beyond, *spread)]:
            here = slice(w0, w0 + chunk)
            half_th = 0.5 * th
            state = jnp.zeros((chunk, main), F32)
            tanhs = []
            for t in range(times):
                now = sh
                for dy in range(TAPS):
                    now = now + part(t, dy, w0)
                y = state + now
                tanh = jnp.tanh(y)
                state = (y + half_th) - half_th * tanh
                tanhs.append(tanh)
            adjoint = jnp.zeros((chunk, main), F32)
            grads, res = [None] * times, [None] * times
            for t in reversed(range(times)):
                slope = 0.5 - 0.5 * (tanhs[t] * tanhs[t])
                up = packed(cot, at_of[t], w0).astype(F32)
                adjoint = adjoint + slope * (up - th * adjoint)
                out = adjoint if keep is None else adjoint * keep
                grads[t] = out.astype(BF16)
                if h is not None:
                    fired = 0.5 + 0.5 * tanhs[t]
                    res[t] = (fired + packed(spike, at_of[t], w0).astype(F32)).astype(BF16)
            mine = core == 0
            for tl in range(steps):
                a, b = grads[tl], grads[steps + tl]
                gk_ref[tl, g, here] = jnp.where(mine, a, b)
                gs_ref[tl, g, here] = jnp.where(mine, b, a)
                if h is not None:
                    a, b = res[tl], res[steps + tl]
                    rk_ref[tl, h, here] = jnp.where(mine, a, b)
                    rs_ref[tl, h, here] = jnp.where(mine, b, a)

    def scan_own(h, strip):
        scan(
            strip,
            lambda at, *here: c_ref[h, at, here[0], here[1]],
            lambda at, *here: s_ref[h, at, here[0], here[1]],
            h + 1,
            h,
        )

    def scan_halo(n, strip, g, keep=None):
        scan(strip, lambda at, *here: halos[n][1][at, here[0], here[1]], None, g, None, keep)

    if two:
        flip = row == 1
        edge_strip = jnp.where(flip, rows + 2, 0)
        edge = jnp.where(flip, rows + 1, 0)
        p_ref[edge_strip] = jnp.zeros(p_ref.shape[1:], F32)
        for ref in (gk_ref, gs_ref):
            for tl in range(steps):
                ref[tl, edge] = jnp.zeros(ref.shape[2:], BF16)

        def scan_at(j):
            if j == rows:
                scan_halo(0, jnp.where(flip, 0, rows), jnp.where(flip, 0, rows + 1))
            elif 0 <= j < rows:
                h = jnp.where(flip, rows - 1 - j, j)
                scan_own(h, jnp.where(flip, h + 1, h))

        done = 0
        for i, (x, h, strip) in enumerate(strips(x_ref, halos[0][0])):
            currents(x, h, strip)
            while done <= 2 * i - 2:
                scan_at(done)
                done += 1
        while done <= rows:
            scan_at(done)
            done += 1
    else:
        last = lax.axis_size("rows") - 1
        currents(halos[0][0], 0, 0)
        currents(halos[1][0], 0, rows + 2)

        def pair(i, carry):
            currents(x_ref, 2 * i, 2 * i + 2)
            return carry

        lax.fori_loop(0, rows // 2, pair, 0)

        def one(h, carry):
            scan_own(h, h + 1)
            return carry

        lax.fori_loop(0, rows, one, 0)
        scan_halo(0, 0, 0, jnp.where(row == 0, 0.0, 1.0))
        scan_halo(1, rows + 1, rows + 1, jnp.where(row == last, 0.0, 1.0))


def forward(two, weights, taps, halo_taps, bias, thr, begun=()):
    x, s, c = taps
    rows, times = s.shape[:2]
    cols, half = x.shape[1] // times, bias.shape[0] // 2
    steps = times // 2
    args = [weights, x, s, c] + [a for pair in halo_taps for a in pair] + [bias, thr, *begun]
    main, tail, _ = split_half(half)
    grad = shape((steps, rows + 2, cols + cols * tail // main, main))
    res = shape((steps, rows, cols + cols * tail // main, main))
    return call(
        functools.partial(forward_kernel, two, bool(begun)),
        (grad, grad, res, res),
        [VMEM_SPEC] * len(args),
        16,
        "forward",
        [pltpu.VMEM((rows + (3 if two else 4), times * cols, weights.shape[0]), F32)],
        cost=24 << 20,
    )(*args)


def unpack(x, cols):
    main = x.shape[2]
    chunk = x.shape[1] - cols
    tail = main * chunk // cols
    parts = [x[:, cols:, k * tail : (k + 1) * tail] for k in range(cols // chunk)]
    return x[:, :cols], jnp.concatenate(parts, axis=1)


def rows_of_grads(g_ref, t, h0, count, cols, padded):
    taps = [unpack(g_ref[t, pl.ds(h0 + 2 - dy, count)], cols) for dy in range(TAPS)]
    mains, tails = ([x[k].reshape(count * cols, -1) for x in taps] for k in range(2))
    rest = jnp.zeros((count * cols, padded - sum(x.shape[1] for x in mains + tails)), BF16)
    return jnp.concatenate(mains + tails + [rest], axis=1)


def backward_own_kernel(w_ref, g_ref, y_ref):
    steps, rows2 = g_ref.shape[:2]
    rows = rows2 - 2
    for t in range(steps):
        grads = rows_of_grads(g_ref, t, 0, rows, y_ref.shape[1] // rows, w_ref.shape[0])
        y_ref[t] = dot(grads, w_ref[...], ((1,), (0,)))


def backward_own(weights, grads, cols):
    steps, rows2 = grads.shape[:2]
    out = shape((steps, (rows2 - 2) * cols, weights.shape[1]), F32)
    return call(backward_own_kernel, out, [VMEM_SPEC] * 2, 12, "backward_own", cost=6 << 20)(weights, grads)


def backward_kernel(w_ref, g_ref, y_ref, cot_ref, rk_ref, rs_ref, out_hbm, res_hbm, out_ref, res_ref, sems):
    steps, rows, cols, ch = cot_ref.shape
    core = lax.axis_index("tm")
    edge = lax.broadcasted_iota(jnp.int32, (1, cols, 1), 1)
    block = 4
    copies = []
    for t in range(steps):
        for h0 in range(0, rows, block):
            total = dot(rows_of_grads(g_ref, t, h0, block, cols, w_ref.shape[0]), w_ref[...], ((1,), (0,)))
            total = (total + y_ref[t, h0 * cols : (h0 + block) * cols, :]).reshape(block, cols, -1)
            left, mid, right = (total[:, :, k * ch : (k + 1) * ch] for k in range(TAPS))
            left = jnp.where(edge == cols - 1, 0.0, pltpu.roll(left, cols - 1, 1))
            right = jnp.where(edge == 0, 0.0, pltpu.roll(right, 1, 1))
            here = t, slice(h0, h0 + block)
            out_ref[here] = cot_ref[here].astype(F32) + (left + mid + right)
            a, b = (jnp.concatenate(unpack(ref[here].astype(F32), cols), axis=2) for ref in (rk_ref, rs_ref))
            both = jnp.concatenate([jnp.where(core == 0, a, b), jnp.where(core == 0, b, a)], axis=2)
            res_ref[here] = both.astype(BF16)
            for n, (ref, hbm) in enumerate(((out_ref, out_hbm), (res_ref, res_hbm))):
                window = t, pl.ds(h0, block)
                copies.append(pltpu.make_async_copy(ref.at[window], hbm.at[window], sems.at[len(copies)]))
                copies[-1].start()
    for copy in copies:
        copy.wait()


def backward(weights, grads, y, cot, res_keep, res_arrived):
    steps, rows = cot.shape[:2]
    return call(
        backward_kernel,
        (shape(cot.shape, F32), shape(cot.shape)),
        [VMEM_SPEC] * 6,
        24,
        "backward",
        [
            pltpu.VMEM(cot.shape, F32),
            pltpu.VMEM(cot.shape, BF16),
            pltpu.SemaphoreType.DMA((2 * steps * (rows // 4),)),
        ],
        out_specs=(pl.BlockSpec(memory_space=pltpu.HBM),) * 2,
    )(weights, grads, y, cot, res_keep, res_arrived)


def swap_cores(x):
    return lax.ppermute(x, "tm", [(0, 1), (1, 0)])


def fetch_halos(two, halos):
    if two:
        return [lax.ppermute(halos[0], "rows", [(0, 1), (1, 0)])]
    count = lax.axis_size("rows")
    head, tail = halos
    return [
        lax.ppermute(tail, "rows", [(i, i + 1) for i in range(count - 1)]),
        lax.ppermute(head, "rows", [(i + 1, i) for i in range(count - 1)]),
    ]


def on_device(spikes, cotangent, weight_codes, block_exponents, current_bias, threshold):
    two = lax.axis_size("rows") == 2
    spikes, cot = spikes[0], cotangent[0]
    w, send, *halos = prepare(two, weight_codes, block_exponents, spikes, cot)
    lanes = QUARTERS * w.shape[2]
    halos = fetch_halos(two, halos)
    taps = build_taps(spikes, cot, swap_cores(spikes), swap_cores(cot), lanes)
    taps, halos = lax.optimization_barrier((taps, halos))
    join, taps, first = fetch_weights(w, send, taps)
    halo_taps = [build_halo_taps(x, swap_cores(x), lanes) for x in halos]
    begun = [first(taps, halo_taps)] if first else []
    w, taps, halo_taps, begun = lax.optimization_barrier((w, taps, halo_taps, begun))
    weights = join(w)
    weights2 = swap_cores(weights)
    keep, send, res_keep, res_send = forward(two, weights, taps, halo_taps, current_bias, threshold, begun)
    arrived = swap_cores(send)
    res_arrived = swap_cores(res_send)
    y = backward_own(weights, keep, cot.shape[2])
    input_grad, residual = backward(weights2, arrived, y, cot, res_keep, res_arrived)
    return residual[None], input_grad[None]


def solution(mesh):
    return jax.shard_map(
        on_device,
        mesh=mesh,
        in_specs=(
            P(("groups", "dp"), "tm", "rows", None, None),
            P(("groups", "dp"), "tm", "rows", None, None),
            P(None, None, None, "dp"),
            P(None, None, None, "dp"),
            P(),
            P(),
        ),
        out_specs=(
            P(("groups", "dp"), "tm", "rows", None, None),
            P(("groups", "dp"), "tm", "rows", None, None),
        ),
        check_vma=False,
    )
```
